32 devices in a mesh: sens: 4 (over y, x), slab: 8 (over z, core).
Axes of the slice: x: 2, y: 2, z: 4, core: 2. Of those that a mesh axis runs over, the one named last changes fastest.
Arguments:
- pressure: bfloat16 [32768, 128], P('slab'), may hold values from 0 to 1
- kernels: bfloat16 [4, 64, 256], replicated, may hold values from -0.0625 to 0.0625
- filter_gains: float32 [512], replicated, may hold values from 0.25 to 2
- measured: float32 [1024, 2, 512], P('sens'), may hold values from -6 to 6
- blocks: int32 [1024, 8, 64], P('sens', 'slab'), may hold values from 0 to 4095
- frames: int32 [1024, 8, 64], P('sens', 'slab'), may hold values from 0 to 2
- classes: int32 [1024, 8, 64], P('sens', 'slab'), may hold values from 0 to 3
- counts: int32 [1024, 8], P('sens', 'slab'), may hold values from 1 to 64, as said below
Outputs:
- residual: float32 [1024, 2, 512], P(('sens', 'slab'))
- gradient: float32 [32768, 128], P('slab', 'sens')
The draws below stay inside these ranges and needn't reach their ends.
Inputs may be any that keep to these rules, and one draw needn't show every extreme that they name: counts[s, j] slots of sensor s in slab j are live; some sensor has all 64 slots live in some slab. `blocks`: slots at or past counts[s, j] are ignored.
All inputs are finite; a program needn't handle non-finite values.
Results may differ from the reference program's by a relative error of at most 0.00077.
Values may be sent and summed in bfloat16 or wider, within the bound.
No kernel may reach another device: no remote copies, remote signals or barrier semaphores. Data moves between devices by JAX's collectives and lax.ppermute only.
A program may use at most 256 MiB of HBM per device.

```python
import math
import jax
import jax.numpy as jnp
from jax import lax

WAVES = 2
VOXELS = 64
KINDS = 4
TIME = 512
FRAME = 128
SLOTS = 64
BLK_DEV = 4096
TAPS = 256
FRAMES = 4
SLABS = 8
SENSORS = 1024
BLOCKS = 32768


def draw_counts(key, part):
    key_weight, key_heavy, key_drop, key_sensor = jax.random.split(key, 4)
    weights = jax.random.randint(key_weight, (SLABS,), 1, 5)
    heavy_slab = jax.random.randint(key_heavy, (), 0, SLABS)
    weights = jnp.where(jnp.arange(SLABS) == heavy_slab, 4, weights)
    dropped = jax.random.randint(key_drop, (SENSORS, SLABS), 0, SLOTS // 4)
    chosen = jax.random.randint(key_sensor, (), 0, SENSORS)
    marked = (jnp.arange(SENSORS)[:, None] == chosen) & (jnp.arange(SLABS)[None, :] == heavy_slab)
    dropped = jnp.where(marked, 0, dropped)
    return jnp.maximum(weights[None, :] * SLOTS // 4 - dropped, 1).astype(jnp.int32)


def set_ends(array, rng, least, top_value):
    longest = array.shape.index(max(array.shape))
    spots = []
    for shift in (0, 1):
        where = [jax.random.randint(jax.random.fold_in(rng, axis), (), 0, length) for axis, length in enumerate(array.shape)]
        where[longest] = (where[longest] + shift) % array.shape[longest]
        spots.append(tuple(where))
    return array.at[spots[0]].set(least).at[spots[1]].set(top_value)


def block_levels(own_key, shape, pieces, least, top_value):
    def one(dim, shards_of):
        heights = jax.random.uniform(jax.random.fold_in(jax.random.fold_in(own_key, 6), dim), (shards_of,), jnp.float32, least / len(pieces), top_value / len(pieces))
        return jnp.repeat(jnp.exp(heights), shape[dim] // shards_of).reshape((-1,) + (1,) * (len(shape) - dim - 1))

    gain = one(*pieces[0])
    for cut in pieces[1:]:
        gain = gain * one(*cut)
    return gain


def normal_values(key, extent, scale, limit, cuts=(), kind=jnp.bfloat16):
    array = jax.random.normal(key, extent, jnp.float32) * scale
    if len(cuts) > 0:
        array = block_levels(key, extent, cuts, -0.22, 0.18) * array
    return jnp.clip(array, min=-limit, max=limit).astype(kind)


def setup_inputs(seed: int = 0) -> dict:
    seeds = jax.random.split(jax.random.key(seed), 9)
    return {
        "pressure": jnp.clip(1.0 * jax.random.uniform(seeds[0], (BLOCKS, WAVES * VOXELS), jnp.float32) ** block_levels(seeds[0], (BLOCKS, WAVES * VOXELS), ((0, 8),), -0.2, 0.2), 0.0, 1.0).astype(jnp.bfloat16),
        "kernels": normal_values(seeds[1], (KINDS, VOXELS, TAPS), (VOXELS * SLOTS * SLABS // 4) ** -0.5, 0.0625),
        "filter_gains": jnp.clip(jnp.exp(jax.random.uniform(seeds[2], (TIME,), jnp.float32, math.log(0.25), math.log(2.0))), 0.25, 2.0),
        "measured": normal_values(seeds[3], (SENSORS, WAVES, TIME), 1.0, 6.0, ((0, 4),), jnp.float32),
        "blocks": set_ends(jax.random.randint(seeds[4], (SENSORS, SLABS, SLOTS), 0, BLK_DEV), jax.random.fold_in(seeds[4], 1), 0, BLK_DEV - 1).astype(jnp.int32),
        "frames": set_ends(jax.random.randint(seeds[5], (SENSORS, SLABS, SLOTS), 0, FRAMES - 1), jax.random.fold_in(seeds[5], 1), 0, (FRAMES - 1) - 1).astype(jnp.int32),
        "classes": set_ends(jax.random.randint(seeds[6], (SENSORS, SLABS, SLOTS), 0, KINDS), jax.random.fold_in(seeds[6], 1), 0, KINDS - 1).astype(jnp.int32),
        "counts": draw_counts(jax.random.fold_in(seeds[8], 71), 0),
    }


def dft_pair():
    sample_ids = jnp.arange(TIME, dtype=jnp.int32)
    phase_ids = (sample_ids[:, None] * sample_ids[None, :]) % TIME
    angles = phase_ids.astype(jnp.float32) * (2.0 * math.pi / TIME)
    return jnp.cos(angles), jnp.sin(angles)


def time_filter(traces, filter_gains, cosine_table, sine_table):
    rows_flat = traces.reshape(-1, TIME)
    real_part = jnp.dot(rows_flat, cosine_table, precision=lax.Precision.HIGHEST, preferred_element_type=jnp.float32) * filter_gains
    imag_part = jnp.dot(rows_flat, sine_table, precision=lax.Precision.HIGHEST, preferred_element_type=jnp.float32) * filter_gains
    result = jnp.dot(real_part, cosine_table, precision=lax.Precision.HIGHEST, preferred_element_type=jnp.float32)
    result = result + jnp.dot(imag_part, sine_table, precision=lax.Precision.HIGHEST, preferred_element_type=jnp.float32)
    return (result / TIME).reshape(traces.shape)


def reference(pressure, kernels, filter_gains, measured, blocks, frames, classes, counts):
    cosine_table, sine_table = dft_pair()
    kern_flat = jnp.transpose(kernels, (1, 0, 2)).reshape(VOXELS, KINDS * TAPS)
    kern_by_tap = jnp.transpose(kernels, (0, 2, 1)).reshape(KINDS * TAPS, VOXELS).astype(jnp.float32)
    slab_ids = jnp.arange(SLABS, dtype=jnp.int32)
    owner_ids = jnp.repeat(jnp.arange(SENSORS, dtype=jnp.int32), SLOTS)
    sensor_grid = jnp.broadcast_to(jnp.arange(SENSORS, dtype=jnp.int32)[:, None], (SENSORS, SLOTS))

    def slab_tables(slab_index):
        block_ids = lax.dynamic_index_in_dim(blocks, slab_index, 1, keepdims=False)
        frame_ids = lax.dynamic_index_in_dim(frames, slab_index, 1, keepdims=False)
        kind_ids = lax.dynamic_index_in_dim(classes, slab_index, 1, keepdims=False)
        live_count = lax.dynamic_index_in_dim(counts, slab_index, 1, keepdims=False)
        live_slot = (jnp.arange(SLOTS, dtype=jnp.int32)[None, :] < live_count[:, None]).astype(jnp.float32)
        return block_ids, frame_ids, kind_ids, live_slot

    def slab_traces(slab_index):
        block_ids, frame_ids, kind_ids, live_slot = slab_tables(slab_index)
        slab_cut = lax.dynamic_slice_in_dim(pressure, slab_index * BLK_DEV, BLK_DEV, 0)
        slab_rows = slab_cut.reshape(BLK_DEV * WAVES, VOXELS)
        projected = jnp.dot(slab_rows, kern_flat, preferred_element_type=jnp.float32).reshape(BLK_DEV, WAVES, KINDS, TAPS)
        shell_terms = projected[block_ids.reshape(-1), :, kind_ids.reshape(-1), :]
        shell_terms = shell_terms * live_slot.reshape(-1)[:, None, None]
        frame_flat = frame_ids.reshape(-1)
        first_part = jax.ops.segment_sum(shell_terms[:, :, :FRAME], owner_ids * FRAMES + frame_flat, num_segments=SENSORS * FRAMES)
        second_part = jax.ops.segment_sum(shell_terms[:, :, FRAME:], owner_ids * FRAMES + frame_flat + 1, num_segments=SENSORS * FRAMES)
        summed = (first_part + second_part).reshape(SENSORS, FRAMES, WAVES, FRAME)
        return jnp.transpose(summed, (0, 2, 1, 3)).reshape(SENSORS, WAVES, TIME)

    traces = jnp.sum(lax.map(slab_traces, slab_ids), axis=0)
    residual = time_filter(traces, filter_gains, cosine_table, sine_table) - measured
    back = time_filter(residual, filter_gains, cosine_table, sine_table).astype(jnp.bfloat16)
    framed = back.reshape(SENSORS, WAVES, FRAMES, FRAME)

    def slab_gradient(slab_index):
        block_ids, frame_ids, kind_ids, live_slot = slab_tables(slab_index)
        low_part = framed[sensor_grid, :, frame_ids, :]
        high_part = framed[sensor_grid, :, frame_ids + 1, :]
        windows = jnp.concatenate([low_part, high_part], axis=-1).astype(jnp.float32) * live_slot[:, :, None, None]
        gathered = jax.ops.segment_sum(windows.reshape(-1, WAVES, TAPS), (block_ids * KINDS + kind_ids).reshape(-1), num_segments=BLK_DEV * KINDS)
        gathered = jnp.transpose(gathered.reshape(BLK_DEV, KINDS, WAVES, TAPS), (0, 2, 1, 3)).reshape(BLK_DEV * WAVES, KINDS * TAPS)
        slab_grad = jnp.dot(gathered, kern_by_tap, precision=lax.Precision.HIGHEST, preferred_element_type=jnp.float32)
        return slab_grad.reshape(BLK_DEV, WAVES * VOXELS)

    gradients = lax.map(slab_gradient, slab_ids)
    gradient = gradients.reshape(BLOCKS, WAVES * VOXELS)
    return residual, gradient
```

```python
import functools
import math

import jax
import jax.numpy as jnp
from jax import lax
from jax.experimental import pallas as pl
from jax.experimental.pallas import tpu as pltpu
from jax.sharding import PartitionSpec as P

LANES = 256
UNIT = 4


def filter_matrix(filter_gains):
    time_len = filter_gains.shape[0]
    sample_ids = jnp.arange(time_len, dtype=jnp.int32)
    phase_ids = sample_ids[:, None] * sample_ids[None, :] % time_len
    angles = phase_ids.astype(jnp.float32) * (2.0 * math.pi / time_len)
    basis = jnp.concatenate([jnp.cos(angles), jnp.sin(angles)], axis=1)
    gains = jnp.concatenate([filter_gains, filter_gains])
    product = lax.dot_general(
        basis * gains,
        basis,
        (((1,), (1,)), ((), ())),
        precision=lax.Precision.HIGHEST,
        preferred_element_type=jnp.float32,
    )
    return product / time_len


def split_parts(array, count):
    parts = []
    for _ in range(count):
        part = array.astype(jnp.bfloat16)
        parts.append(part)
        array = array - part.astype(jnp.float32)
    return parts


def forward_kernel(
    kinds, places, code_ref, pressure_ref, kernel_ref, tally_ref, traces_ref, grouped_ref
):
    combos = kinds * places
    rows = UNIT * combos
    blocks = pressure_ref.shape[0]
    tops = blocks // LANES
    units = code_ref.shape[0]
    sensors = units * UNIT
    slots = code_ref.shape[1]
    voxels = pressure_ref.shape[1] // 2
    frame = kernel_ref.shape[1] // 2

    def unit_step(unit, _):
        code = code_ref[pl.ds(unit, 1), :]
        row_code = lax.shift_right_arithmetic(code, 8)
        low_code = code & (LANES - 1)
        row_hot = (lax.broadcasted_iota(jnp.int32, (tops * rows, slots), 0) == row_code).astype(
            jnp.bfloat16
        )
        low_hot = (lax.broadcasted_iota(jnp.int32, (LANES, slots), 0) == low_code).astype(
            jnp.bfloat16
        )
        tally = lax.dot_general(
            row_hot, low_hot, (((1,), (1,)), ((), ())), preferred_element_type=jnp.float32
        ).astype(jnp.bfloat16)
        base = pl.multiple_of(unit * rows, rows)
        for top in range(tops):
            tally_ref[pl.ds(base, rows), top * LANES : (top + 1) * LANES] = tally[
                top * rows : (top + 1) * rows
            ]
        return 0

    lax.fori_loop(0, units, unit_step, 0)
    grouped_ref[...] = jnp.dot(
        tally_ref[...], pressure_ref[...], preferred_element_type=jnp.float32
    )
    sums = [None] * (places + 1)
    for place in range(places):
        picked = [
            grouped_ref[pl.ds(place * kinds + kind, sensors, stride=combos), :]
            for kind in range(kinds)
        ]
        wide = jnp.concatenate(
            [
                jnp.concatenate([g[:, w * voxels : (w + 1) * voxels] for g in picked], axis=1)
                for w in range(2)
            ],
            axis=0,
        )
        taps = jnp.dot(
            jnp.concatenate(split_parts(wide, 3), axis=0),
            kernel_ref[...],
            preferred_element_type=jnp.float32,
        )
        count = 2 * sensors
        taps = taps[:count] + (taps[count : 2 * count] + taps[2 * count :])
        for half in range(2):
            piece = taps[:, half * frame : (half + 1) * frame]
            spot = place + half
            sums[spot] = piece if sums[spot] is None else sums[spot] + piece
    total = jnp.concatenate(sums, axis=1)
    time_len = total.shape[1]
    for w in range(2):
        traces_ref[:, w * time_len : (w + 1) * time_len] = total[w * sensors : (w + 1) * sensors]


def forward(code, pressure, kern_rows, kinds, places, time_len, steps):
    units = code.shape[0]
    sensors = units * UNIT
    combos = kinds * places
    per_step = units // steps
    block_count = pressure.shape[0]
    return pl.pallas_call(
        functools.partial(forward_kernel, kinds, places),
        grid=(steps,),
        in_specs=[
            pl.BlockSpec((per_step, code.shape[1]), lambda i: (i, 0)),
            pl.BlockSpec(pressure.shape, lambda i: (0, 0)),
            pl.BlockSpec(kern_rows.shape, lambda i: (0, 0)),
        ],
        out_specs=[
            pl.BlockSpec((per_step * UNIT * combos, block_count), lambda i: (i, 0)),
            pl.BlockSpec((per_step * UNIT, 2 * time_len), lambda i: (i, 0)),
        ],
        out_shape=[
            jax.ShapeDtypeStruct((sensors * combos, block_count), jnp.bfloat16),
            jax.ShapeDtypeStruct((sensors, 2 * time_len), jnp.float32),
        ],
        scratch_shapes=[pltpu.VMEM((per_step * UNIT * combos, pressure.shape[1]), jnp.float32)],
        compiler_params=pltpu.CompilerParams(
            dimension_semantics=("arbitrary",), vmem_limit_bytes=56 << 20
        ),
        name="forward",
    )(code, pressure, kern_rows)


def backward_kernel(kinds, places, back_ref, kernel_ref, tally_ref, grad_ref, wide_ref, resp_ref):
    combos = kinds * places
    sensors = back_ref.shape[0]
    time_len = back_ref.shape[1] // 2
    taps = kernel_ref.shape[1]
    frame = taps // 2
    width = wide_ref.shape[1]
    voxels = width // 2

    @pl.when(pl.program_id(0) == 0)
    def _():
        for place in range(places):
            waves = []
            for w in range(2):
                start = w * time_len + place * frame
                waves.append(
                    lax.dot_general(
                        back_ref[:, start : start + taps],
                        kernel_ref[...],
                        (((1,), (1,)), ((), ())),
                        preferred_element_type=jnp.float32,
                    )
                )
            for kind in range(kinds):
                cut = slice(kind * voxels, (kind + 1) * voxels)
                wide_ref[pl.ds(place * kinds + kind, sensors, stride=combos), :] = jnp.concatenate(
                    [waves[0][:, cut], waves[1][:, cut]], axis=1
                )
        flipped = wide_ref[...].T
        high, low = split_parts(flipped, 2)
        resp_ref[:width] = high
        resp_ref[width:] = low

    both = jnp.dot(resp_ref[...], tally_ref[...], preferred_element_type=jnp.float32)
    grad_ref[...] = both[:width] + both[width:]


def backward(back, kern_rows, tally, kinds, places, width, steps):
    rows, block_count = tally.shape
    cut = block_count // steps
    return pl.pallas_call(
        functools.partial(backward_kernel, kinds, places),
        grid=(steps,),
        in_specs=[
            pl.BlockSpec(back.shape, lambda i: (0, 0)),
            pl.BlockSpec(kern_rows.shape, lambda i: (0, 0)),
            pl.BlockSpec((rows, cut), lambda i: (0, i)),
        ],
        out_specs=pl.BlockSpec((width, cut), lambda i: (0, i)),
        out_shape=jax.ShapeDtypeStruct((width, block_count), jnp.float32),
        scratch_shapes=[
            pltpu.VMEM((rows, width), jnp.float32),
            pltpu.VMEM((2 * width, rows), jnp.bfloat16),
        ],
        compiler_params=pltpu.CompilerParams(
            dimension_semantics=("arbitrary",), vmem_limit_bytes=56 << 20
        ),
        name="backward",
    )(back, kern_rows, tally)


def scatter_slab(partial):
    slabs = lax.axis_size("slab")
    chips = slabs // 2
    place = lax.axis_index("slab")
    core = place % 2
    chip = place // 2
    rows = partial.reshape(chips, 2, partial.shape[0] // slabs, partial.shape[1])
    mine = lax.dynamic_index_in_dim(rows, core, 1, keepdims=False)
    other = lax.dynamic_index_in_dim(rows, 1 - core, 1, keepdims=False)
    paired = mine + lax.ppermute(other, "slab", [(j, j ^ 1) for j in range(slabs)])
    total = lax.dynamic_index_in_dim(paired, chip, 0, keepdims=False)
    for step in range(1, chips):
        block = lax.dynamic_index_in_dim(paired, (chip + step) % chips, 0, keepdims=False)
        total = total + lax.ppermute(
            block, "slab", [(j, (j + 2 * step) % slabs) for j in range(slabs)]
        )
    return total


def gather_slab(share):
    return lax.all_gather(share, "slab", axis=0, tiled=True)


def scatter_sens(partial):
    groups = lax.axis_size("sens")
    own = lax.axis_index("sens")
    blocks = partial.reshape(groups, partial.shape[0] // groups, partial.shape[1])
    total = lax.dynamic_index_in_dim(blocks, own, 0, keepdims=False)
    for step in range(1, groups):
        block = lax.dynamic_index_in_dim(blocks, own ^ step, 0, keepdims=False)
        total = total + lax.ppermute(block, "sens", [(q, q ^ step) for q in range(groups)])
    return total


def per_device(pressure, kernels, filter_gains, measured, blocks, frames, classes, counts):
    kinds, voxels, taps = kernels.shape
    block_count, width = pressure.shape
    frame = taps // 2
    time_len = filter_gains.shape[0]
    places = time_len // frame - 1
    combos = kinds * places
    sensors, slots = blocks.shape[0], blocks.shape[2]
    share = sensors // lax.axis_size("slab")

    block_ids = blocks[:, 0, :]
    combo_ids = frames[:, 0, :] * kinds + classes[:, 0, :]
    live = jnp.arange(slots, dtype=jnp.int32)[None, :] < counts
    lane = jnp.arange(sensors, dtype=jnp.int32)[:, None] % UNIT
    row_code = (block_ids // LANES) * (UNIT * combos) + lane * combos + combo_ids
    code = jnp.where(live, row_code * LANES + block_ids % LANES, -LANES)
    code = code.reshape(sensors // UNIT, UNIT * slots)
    kern_rows = kernels.reshape(kinds * voxels, taps)

    tally, partial = forward(code, pressure, kern_rows, kinds, places, time_len, 4)
    traces = scatter_slab(partial).reshape(share * 2, time_len)
    matrix = filter_matrix(filter_gains)
    measured_share = lax.dynamic_slice_in_dim(measured, lax.axis_index("slab") * share, share, 0)
    dot = functools.partial(
        jnp.dot, precision=lax.Precision.HIGHEST, preferred_element_type=jnp.float32
    )
    residual = dot(traces, matrix) - measured_share.reshape(share * 2, time_len)
    back = dot(residual, matrix).astype(jnp.bfloat16)
    back_all = gather_slab(back.reshape(share, 2 * time_len))
    grad = backward(back_all, kern_rows, tally, kinds, places, width, 4)
    gradient = scatter_sens(grad).T
    return (residual.reshape(share, 2, time_len), gradient)


def solution(mesh):
    return jax.shard_map(
        per_device,
        mesh=mesh,
        in_specs=(
            P("slab", None),
            P(),
            P(),
            P("sens", None, None),
            P("sens", "slab", None),
            P("sens", "slab", None),
            P("sens", "slab", None),
            P("sens", "slab"),
        ),
        out_specs=(P(("sens", "slab"), None, None), P("slab", "sens")),
        check_vma=False,
    )
```

```python
import functools
import math

import jax
import jax.numpy as jnp
import numpy as np
from jax import lax
from jax.experimental import pallas as pl
from jax.experimental.pallas import tpu as pltpu
from jax.sharding import PartitionSpec as P

LANES = 256
UNIT = 4
HOT = jnp.float8_e4m3fn
CODE = 32766.0
TINY = 1e-37
RATE = 256 / math.log(2.0)
GRAIN = 256
PARTS = 2


def in_hbm(array):
    return pltpu.with_memory_space_constraint(array, pltpu.HBM)


def to_bf16(array):
    return array.astype(jnp.float32).astype(jnp.bfloat16)


def filter_kernel(gains_ref, cosine_ref, matrix_ref):
    time_len = cosine_ref.shape[0]
    row = jnp.dot(
        jnp.broadcast_to(gains_ref[...], (8, time_len)),
        cosine_ref[...],
        precision=lax.Precision.HIGHEST,
        preferred_element_type=jnp.float32,
    )
    wide = jnp.broadcast_to(row[:1] / time_len, (time_len, time_len))
    matrix_ref[...] = pltpu.roll(wide, 0, axis=1, stride=1, stride_axis=0)


def filter_matrix(filter_gains):
    time_len = filter_gains.shape[0]
    ids = np.arange(time_len)
    cosine = np.cos(np.outer(ids, ids) % time_len * (2.0 * math.pi / time_len))
    return pl.pallas_call(
        filter_kernel,
        out_shape=pltpu.VMEM((time_len, time_len), jnp.float32),
        compiler_params=pltpu.CompilerParams(vmem_limit_bytes=8 << 20),
        name="filter_matrix",
    )(filter_gains[None, :], jnp.asarray(cosine, jnp.float32))


def split_parts(array, count):
    parts = []
    for _ in range(count):
        part = array.astype(jnp.bfloat16)
        parts.append(part)
        array = array - part.astype(jnp.float32)
    return parts


def forward_kernel(
    kinds,
    places,
    core_ref,
    blocks_hbm,
    frames_hbm,
    classes_hbm,
    counts_hbm,
    pressure_hbm,
    kernel_hbm,
    *refs,
):
    tally_hbms = refs[:PARTS]
    (
        mine_ref,
        other_ref,
        blocks_ref,
        frames_ref,
        classes_ref,
        counts_ref,
        pressure_ref,
        kernel_ref,
        tally_ref,
        code_ref,
        grouped_ref,
        in_sems,
        out_sems,
    ) = refs[PARTS:]
    loads = [
        pltpu.make_async_copy(source, target, in_sems.at[spot])
        for spot, (source, target) in enumerate(
            (
                (blocks_hbm, blocks_ref),
                (frames_hbm, frames_ref),
                (classes_hbm, classes_ref),
                (counts_hbm, counts_ref),
                (pressure_hbm, pressure_ref),
                (kernel_hbm, kernel_ref),
            )
        )
    ]
    for load in loads:
        load.start()
    for load in loads[:4]:
        load.wait()
    combos = kinds * places
    rows = UNIT * combos
    block_count = pressure_ref.shape[0]
    tops = block_count // LANES
    slots, sensors = blocks_ref.shape
    units = sensors // UNIT
    voxels = pressure_ref.shape[1] // 2
    frame = kernel_ref.shape[1] // 2

    block_ids = blocks_ref[...]
    lane = lax.broadcasted_iota(jnp.int32, (slots, sensors), 1) // units
    row_ids = lane * combos + frames_ref[...] * kinds + classes_ref[...]
    live = lax.broadcasted_iota(jnp.int32, (slots, sensors), 0) < counts_ref[...]
    code = jnp.where(live, row_ids * block_count + block_ids, -1).T
    code_ref[...] = jnp.concatenate(
        [code[part * units : (part + 1) * units] for part in range(UNIT)], axis=1
    )

    width = UNIT * slots
    row_iota = to_bf16(lax.broadcasted_iota(jnp.int32, (rows, width), 0))
    low_iota = to_bf16(lax.broadcasted_iota(jnp.int32, (LANES, width), 0))
    one, zero = jnp.ones((), jnp.bfloat16), jnp.zeros((), jnp.bfloat16)

    def unit_step(unit, _):
        code = code_ref[pl.ds(unit, 1), :]
        row_code = lax.div(code, block_count)
        block_code = code & (block_count - 1)
        top_code = jnp.where(code < 0, -1, lax.div(block_code, LANES))
        low_code = to_bf16(block_code & (LANES - 1))
        row_hot = []
        for top in range(tops):
            picked = to_bf16(jnp.where(top_code == top, row_code, -1))
            row_hot.append(jnp.where(row_iota == picked, one, zero))
        row_hot = jnp.concatenate(row_hot, axis=0).astype(HOT)
        low_hot = jnp.where(low_iota == low_code, one, zero).astype(HOT)
        tally = lax.dot_general(
            row_hot, low_hot, (((1,), (1,)), ((), ())), preferred_element_type=jnp.float32
        ).astype(jnp.bfloat16)
        base = pl.multiple_of(unit * rows, rows)
        for top in range(tops):
            tally_ref[pl.ds(base, rows), top * LANES : (top + 1) * LANES] = tally[
                top * rows : (top + 1) * rows
            ]
        return 0

    chunks = out_sems.shape[0]
    span = units // chunks
    stores = []
    for chunk in range(chunks):
        lax.fori_loop(chunk * span, (chunk + 1) * span, unit_step, 0, unroll=4)
        part = pl.ds(chunk * span * rows, span * rows)
        for spot, tally_hbm in enumerate(tally_hbms):
            width = tally_hbm.shape[1]
            store = pltpu.make_async_copy(
                tally_ref.at[part, pl.ds(spot * width, width)],
                tally_hbm.at[part],
                out_sems.at[chunk, spot],
            )
            store.start()
            stores.append(store)
    for load in loads[4:]:
        load.wait()
    grouped_ref[...] = jnp.dot(
        tally_ref[...], pressure_ref[...], preferred_element_type=jnp.float32
    )
    core = core_ref[0]
    share = mine_ref.shape[1]
    for part in range(UNIT):
        sums = [None] * (places + 1)
        for place in range(places):
            first = part * combos + place * kinds
            picked = [
                grouped_ref[pl.ds(first + kind, units, stride=rows), :] for kind in range(kinds)
            ]
            wide = jnp.concatenate(
                [
                    jnp.concatenate([g[:, w * voxels : (w + 1) * voxels] for g in picked], axis=1)
                    for w in range(2)
                ],
                axis=0,
            )
            taps = jnp.dot(
                jnp.concatenate(split_parts(wide, 3), axis=0),
                kernel_ref[...],
                preferred_element_type=jnp.float32,
            )
            count = 2 * units
            taps = taps[:count] + (taps[count : 2 * count] + taps[2 * count :])
            for half in range(2):
                piece = taps[:, half * frame : (half + 1) * frame]
                spot = place + half
                sums[spot] = piece if sums[spot] is None else sums[spot] + piece
        total = jnp.concatenate(sums, axis=1)
        total = jnp.concatenate([total[:units], total[units:]], axis=1)
        pairs = units // (2 * share)
        for pair in range(pairs):
            even = total[2 * pair * share : (2 * pair + 1) * share]
            odd = total[(2 * pair + 1) * share : (2 * pair + 2) * share]
            mine_ref[part * pairs + pair] = jnp.where(core == 0, even, odd)
            other_ref[part * pairs + pair] = jnp.where(core == 0, odd, even)
    for store in stores:
        store.wait()


def forward(blocks, frames, classes, counts, pressure, kern_rows, kinds, places, time_len):
    slots, sensors = blocks.shape
    combos = kinds * places
    block_count = pressure.shape[0]
    slabs = lax.axis_size("slab")
    core = (lax.axis_index("slab") % 2).reshape(1)
    anywhere = pl.BlockSpec(memory_space=pltpu.HBM)
    vmem = pl.BlockSpec(memory_space=pltpu.VMEM)
    half = (slabs // 2, sensors // slabs, 2 * time_len)
    tally = jax.ShapeDtypeStruct((sensors * combos, block_count // PARTS), jnp.bfloat16)
    operands = (blocks, frames, classes, counts, pressure, kern_rows)
    *tallies, mine, other = pl.pallas_call(
        functools.partial(forward_kernel, kinds, places),
        in_specs=[pl.BlockSpec(memory_space=pltpu.SMEM)] + [anywhere] * 6,
        out_specs=[anywhere] * PARTS + [vmem, vmem],
        out_shape=[tally] * PARTS
        + [
            jax.ShapeDtypeStruct(half, jnp.float32),
            jax.ShapeDtypeStruct(half, jnp.float32),
        ],
        scratch_shapes=[pltpu.VMEM(operand.shape, operand.dtype) for operand in operands]
        + [
            pltpu.VMEM((tally.shape[0], block_count), tally.dtype),
            pltpu.VMEM((sensors // UNIT, UNIT * slots), jnp.int32),
            pltpu.VMEM((sensors * combos, pressure.shape[1]), jnp.float32),
            pltpu.SemaphoreType.DMA((len(operands),)),
            pltpu.SemaphoreType.DMA((8, PARTS)),
        ],
        compiler_params=pltpu.CompilerParams(vmem_limit_bytes=48 << 20),
        name="forward",
    )(core, *[in_hbm(operand) for operand in operands])
    return tallies, mine, other


def fill_responses(kinds, places, order_ref, piece_refs, kernel_ref, resp_ref, back_ref, wide_ref):
    combos = kinds * places
    rows = UNIT * combos
    share = piece_refs[0].shape[0]
    sensors = back_ref.shape[0]
    units = sensors // UNIT
    time_len = back_ref.shape[1] // 2
    taps = kernel_ref.shape[1]
    frame = taps // 2
    width = wide_ref.shape[1]
    voxels = width // 2
    for spot, piece_ref in enumerate(piece_refs):
        start = pl.multiple_of(order_ref[spot] * share, share)
        back_ref[pl.ds(start, share), :] = piece_ref[...]
    for place in range(places):
        waves = []
        for w in range(2):
            start = w * time_len + place * frame
            waves.append(
                lax.dot_general(
                    back_ref[:, start : start + taps],
                    kernel_ref[...],
                    (((1,), (1,)), ((), ())),
                    preferred_element_type=jnp.float32,
                )
            )
        for kind in range(kinds):
            cut = slice(kind * voxels, (kind + 1) * voxels)
            both = jnp.concatenate([waves[0][:, cut], waves[1][:, cut]], axis=1)
            for part in range(UNIT):
                first = part * combos + place * kinds + kind
                wide_ref[pl.ds(first, units, stride=rows), :] = both[
                    part * units : (part + 1) * units
                ]
    high, low = split_parts(wide_ref[...].T, 2)
    resp_ref[:width] = high
    resp_ref[width:] = low


def backward_kernel(kinds, places, pieces, own_ref, tally_hbm, *refs):
    if pieces:
        order_ref, *piece_refs = refs[: pieces + 1]
        kernel_ref, resp_ref, kept_ref, *code_refs = refs[pieces + 1 : -5]
        tally_ref, grad_ref, sems, back_ref, wide_ref = refs[-5:]
    else:
        resp_ref, kept_ref, *code_refs = refs[:-3]
        tally_ref, grad_ref, sems = refs[-3:]
    groups, share, span = grad_ref.shape
    cuts = sems.shape[0]
    loads = []
    for cut in range(cuts):
        here = pl.ds(cut * (span // cuts), span // cuts)
        loads.append(
            pltpu.make_async_copy(tally_hbm.at[:, here], tally_ref.at[:, here], sems.at[cut])
        )
        loads[-1].start()
    if pieces:
        fill_responses(
            kinds, places, order_ref, piece_refs, kernel_ref, resp_ref, back_ref, wide_ref
        )
    width = groups * share
    for cut, load in enumerate(loads):
        load.wait()
        here = slice(cut * (span // cuts), (cut + 1) * (span // cuts))
        both = jnp.dot(resp_ref[...], tally_ref[:, here], preferred_element_type=jnp.float32)
        both = both[:width] + both[width:]
        for group in range(groups):
            grad_ref[group, :, here] = both[group * share : (group + 1) * share]
    own = own_ref[0]
    kept_ref[...] = grad_ref[own]
    lanes = code_refs[0].shape[1] - span
    lane = lax.broadcasted_iota(jnp.int32, (share, lanes), 1)
    for step, code_ref in enumerate(code_refs, 1):
        levels = jnp.zeros((share, lanes), jnp.int32)
        for spot in range(span // GRAIN):
            cut = slice(spot * GRAIN, (spot + 1) * GRAIN)
            block = grad_ref[own ^ step, :, cut]
            top = jnp.maximum(jnp.max(jnp.abs(block), axis=1, keepdims=True), TINY)
            level = jnp.minimum(jnp.floor(jnp.log(top) * RATE) + 2.0, CODE)
            code = block * jnp.exp(level * (-1.0 / RATE)) * CODE
            code_ref[:, cut] = jnp.floor(code + 0.5).astype(jnp.int32).astype(jnp.int16)
            levels = jnp.where(lane == spot, level.astype(jnp.int32), levels)
        code_ref[:, span:] = levels.astype(jnp.int16)


def backward(own, tally, width, resp=None, order=None, pieces=(), kern_rows=None, combos=None):
    groups = lax.axis_size("sens")
    share, (rows, span) = width // groups, tally.shape
    vmem = pl.BlockSpec(memory_space=pltpu.VMEM)
    smem = pl.BlockSpec(memory_space=pltpu.SMEM)
    hbm = pl.BlockSpec(memory_space=pltpu.HBM)
    out_shape = [jax.ShapeDtypeStruct((share, span), jnp.float32)] + [
        jax.ShapeDtypeStruct((share, span + 128), jnp.int16)
    ] * (groups - 1)
    scratch = [
        pltpu.VMEM((rows, span), tally.dtype),
        pltpu.VMEM((groups, share, span), jnp.float32),
        pltpu.SemaphoreType.DMA((4,)),
    ]
    if resp is None:
        operands = (order, *pieces, kern_rows)
        specs = [smem] + [vmem] * (len(pieces) + 1)
        out_shape = [jax.ShapeDtypeStruct((2 * width, rows), jnp.bfloat16)] + out_shape
        length = pieces[0].shape[1]
        sensors = pieces[0].shape[0] * len(pieces)
        scratch += [
            pltpu.VMEM((sensors, length), jnp.bfloat16),
            pltpu.VMEM((rows, width), jnp.float32),
        ]
    else:
        operands, specs = (resp,), [vmem]
    outs = pl.pallas_call(
        functools.partial(backward_kernel, *(combos or (0, 0)), len(pieces)),
        in_specs=[smem, hbm] + specs,
        out_specs=[vmem] * len(out_shape),
        out_shape=out_shape,
        scratch_shapes=scratch,
        compiler_params=pltpu.CompilerParams(vmem_limit_bytes=32 << 20),
        cost_estimate=pl.CostEstimate(
            flops=4 * width * rows * span, bytes_accessed=2 * rows * span, transcendentals=0
        ),
        name="backward",
    )(own, in_hbm(tally), *operands)
    if resp is None:
        resp, *outs = outs
    kept, *codes = outs
    received = []
    for step, code in enumerate(codes, 1):
        received.append(lax.ppermute(code, "sens", [(q, q ^ step) for q in range(groups)]))
    return resp, [kept, *received]


def finish_kernel(*refs):
    part_refs, out_ref = refs[:-1], refs[-1]
    count = len(part_refs) // PARTS
    for part in range(PARTS):
        kept_ref, *code_refs = part_refs[part * count : (part + 1) * count]
        span = kept_ref.shape[1]
        for spot in range(span // GRAIN):
            cut = slice(spot * GRAIN, (spot + 1) * GRAIN)
            total = kept_ref[:, cut]
            for code_ref in code_refs:
                level = code_ref[:, span:].astype(jnp.int32).astype(jnp.float32)[:, spot : spot + 1]
                scale = jnp.exp(level * (1.0 / RATE)) * (1.0 / CODE)
                total = total + code_ref[:, cut].astype(jnp.int32).astype(jnp.float32) * scale
            start = part * span + spot * GRAIN
            out_ref[:, start : start + GRAIN] = total


def finish(parts):
    share, span = parts[0].shape
    return pl.pallas_call(
        finish_kernel,
        out_shape=jax.ShapeDtypeStruct((share, PARTS * span), jnp.float32),
        compiler_params=pltpu.CompilerParams(vmem_limit_bytes=8 << 20),
        name="finish",
    )(*parts)


def scatter_slab(mine, other, gains):
    slabs = lax.axis_size("slab")
    chips = slabs // 2
    place = lax.axis_index("slab")
    chip = place // 2
    paired = mine + lax.ppermute(other, "slab", [(j, j ^ 1) for j in range(slabs)])
    paired, gains = lax.optimization_barrier((paired, gains))
    total = lax.dynamic_index_in_dim(paired, chip, 0, keepdims=False)
    for step in (2, 1, 3) if chips == 4 else range(1, chips):
        block = lax.dynamic_index_in_dim(paired, chip ^ step, 0, keepdims=False)
        total = total + lax.ppermute(block, "slab", [(j, j ^ (2 * step)) for j in range(slabs)])
    return total, gains


def gather_slab(share):
    slabs = lax.axis_size("slab")
    place = lax.axis_index("slab")
    pieces, order = [share], [place]
    for step in range(1, slabs // 2):
        pieces.append(lax.ppermute(share, "slab", [(j, j ^ (2 * step)) for j in range(slabs)]))
        order.append(place ^ (2 * step))
    for spot in range(slabs // 2):
        pieces.append(lax.ppermute(pieces[spot], "slab", [(j, j ^ 1) for j in range(slabs)]))
        order.append(order[spot] ^ 1)
    return pieces, jnp.stack(order).astype(jnp.int32)


def per_device(pressure, kernels, filter_gains, measured, blocks, frames, classes, counts):
    kinds, voxels, taps = kernels.shape
    block_count, width = pressure.shape
    frame = taps // 2
    time_len = filter_gains.shape[0]
    places = time_len // frame - 1
    combos = kinds * places
    sensors, slots = blocks.shape[0], blocks.shape[2]
    share = sensors // lax.axis_size("slab")

    kern_rows = kernels.reshape(kinds * voxels, taps)

    tallies, mine, other = forward(
        blocks[:, 0, :].T,
        frames[:, 0, :].T,
        classes[:, 0, :].T,
        counts.T,
        pressure,
        kern_rows,
        kinds,
        places,
        time_len,
    )
    traces, gains = scatter_slab(mine, other, filter_gains)
    traces = traces.reshape(share * 2, time_len)
    matrix = filter_matrix(gains)
    measured_share = lax.dynamic_slice_in_dim(measured, lax.axis_index("slab") * share, share, 0)
    dot = functools.partial(
        jnp.dot, precision=lax.Precision.HIGHEST, preferred_element_type=jnp.float32
    )
    residual = dot(traces, matrix) - measured_share.reshape(share * 2, time_len)
    back = dot(residual, matrix).astype(jnp.bfloat16)
    back = back.reshape(share, 2 * time_len)
    pieces, order = gather_slab(back)
    own = lax.axis_index("sens").reshape(1)
    resp, parts = backward(
        own, tallies[0], width, None, order, pieces, kern_rows, (kinds, places)
    )
    for tally in tallies[1:]:
        parts = parts + backward(own, tally, width, resp)[1]
    gradient = finish(parts).T
    return (residual.reshape(share, 2, time_len), gradient)


def solution(mesh):
    return jax.shard_map(
        per_device,
        mesh=mesh,
        in_specs=(
            P("slab", None),
            P(),
            P(),
            P("sens", None, None),
            P("sens", "slab", None),
            P("sens", "slab", None),
            P("sens", "slab", None),
            P("sens", "slab"),
        ),
        out_specs=(P(("sens", "slab"), None, None), P("slab", "sens")),
        check_vma=False,
    )
```

```python
import functools
import math

import jax
import jax.numpy as jnp
import numpy as np
from jax import lax
from jax.experimental import pallas as pl
from jax.experimental.pallas import tpu as pltpu
from jax.sharding import PartitionSpec as P

LANES = 256
UNIT = 4
HOT = jnp.float8_e4m3fn
CODE = 32766.0
TINY = 1e-37
RATE = 256 / math.log(2.0)
GRAIN = 256
SPANS = (4, 4)
CUT = 512


def in_hbm(array):
    return pltpu.with_memory_space_constraint(array, pltpu.HBM)


def to_bf16(array):
    return array.astype(jnp.float32).astype(jnp.bfloat16)


def filter_kernel(gains_hbm, cosine_hbm, kernel_hbm, matrix_ref, fast_ref, *refs):
    gains_ref, cosine_ref, sems = refs
    pairs = [(gains_hbm, gains_ref), (cosine_hbm, cosine_ref), (kernel_hbm, fast_ref)]
    copies = [
        pltpu.make_async_copy(source, target, sems.at[spot])
        for spot, (source, target) in enumerate(pairs)
    ]
    for copy in copies:
        copy.start()
    for copy in copies[:2]:
        copy.wait()
    time_len = cosine_ref.shape[0]
    row = jnp.dot(
        jnp.broadcast_to(gains_ref[...], (8, time_len)),
        cosine_ref[...],
        precision=lax.Precision.HIGHEST,
        preferred_element_type=jnp.float32,
    )
    wide = jnp.broadcast_to(row[:1] / time_len, (time_len, time_len))
    matrix_ref[...] = pltpu.roll(wide, 0, axis=1, stride=1, stride_axis=0)
    for copy in copies[2:]:
        copy.wait()


def filter_matrix(filter_gains, kern_rows):
    time_len = filter_gains.shape[0]
    ids = np.arange(time_len)
    cosine = np.cos(np.outer(ids, ids) % time_len * (2.0 * math.pi / time_len))
    operands = (filter_gains[None, :], jnp.asarray(cosine, jnp.float32), kern_rows)
    return pl.pallas_call(
        filter_kernel,
        in_specs=[pl.BlockSpec(memory_space=pltpu.HBM)] * 3,
        out_specs=[pl.BlockSpec(memory_space=pltpu.VMEM)] * 2,
        out_shape=[
            pltpu.VMEM((time_len, time_len), jnp.float32),
            pltpu.VMEM(kern_rows.shape, kern_rows.dtype),
        ],
        scratch_shapes=[
            pltpu.VMEM((1, time_len), jnp.float32),
            pltpu.VMEM((time_len, time_len), jnp.float32),
            pltpu.SemaphoreType.DMA((3,)),
        ],
        compiler_params=pltpu.CompilerParams(vmem_limit_bytes=8 << 20),
        name="filter_matrix",
    )(*[in_hbm(operand) for operand in operands])


def split_parts(array, count):
    parts = []
    for _ in range(count):
        part = array.astype(jnp.bfloat16)
        parts.append(part)
        array = array - part.astype(jnp.float32)
    return parts


def forward_kernel(
    kinds,
    places,
    core_ref,
    blocks_hbm,
    frames_hbm,
    classes_hbm,
    counts_hbm,
    pressure_hbm,
    kernel_hbm,
    *refs,
):
    tally_hbms = refs[: len(SPANS)]
    (
        mine_ref,
        other_ref,
        blocks_ref,
        frames_ref,
        classes_ref,
        counts_ref,
        pressure_ref,
        kernel_ref,
        tally_ref,
        code_ref,
        grouped_ref,
        in_sems,
        out_sems,
    ) = refs[len(SPANS) :]
    loads = [
        pltpu.make_async_copy(source, target, in_sems.at[spot])
        for spot, (source, target) in enumerate(
            (
                (blocks_hbm, blocks_ref),
                (frames_hbm, frames_ref),
                (classes_hbm, classes_ref),
                (counts_hbm, counts_ref),
                (pressure_hbm, pressure_ref),
                (kernel_hbm, kernel_ref),
            )
        )
    ]
    for load in loads:
        load.start()
    for load in loads[:4]:
        load.wait()
    combos = kinds * places
    rows = UNIT * combos
    block_count = pressure_ref.shape[0]
    tops = block_count // LANES
    slots, sensors = blocks_ref.shape
    units = sensors // UNIT
    voxels = pressure_ref.shape[1] // 2
    frame = kernel_ref.shape[1] // 2

    block_ids = blocks_ref[...]
    lane = lax.broadcasted_iota(jnp.int32, (slots, sensors), 1) // units
    row_ids = lane * combos + frames_ref[...] * kinds + classes_ref[...]
    live = lax.broadcasted_iota(jnp.int32, (slots, sensors), 0) < counts_ref[...]
    code = jnp.where(live, row_ids * block_count + block_ids, -1).T
    code_ref[...] = jnp.concatenate(
        [code[part * units : (part + 1) * units] for part in range(UNIT)], axis=1
    )

    width = UNIT * slots
    step = 16
    row_iota = to_bf16(lax.broadcasted_iota(jnp.int32, (rows, width), 0))
    low_iota = to_bf16(lax.broadcasted_iota(jnp.int32, (LANES, width), 0))
    one, zero = jnp.ones((), jnp.bfloat16), jnp.zeros((), jnp.bfloat16)
    shift = LANES.bit_length() - 1
    depth = block_count.bit_length() - 1

    def unit_step(unit, _):
        code = code_ref[pl.ds(unit, 1), :]
        row_code = to_bf16(lax.shift_right_arithmetic(code, depth))
        top_code = to_bf16(lax.shift_right_arithmetic(code & (block_count - 1), shift))
        low_code = to_bf16(code & (LANES - 1))
        picked = jnp.where(row_iota == row_code, one, zero)
        top_code = jnp.broadcast_to(top_code, (step, width))
        row_hot = []
        for top in range(tops):
            here = top_code == jnp.bfloat16(top)
            for cut in range(0, rows, step):
                row_hot.append(jnp.where(here, picked[cut : cut + step], zero))
        row_hot = jnp.concatenate(row_hot, axis=0).astype(HOT)
        low_hot = jnp.where(low_iota == low_code, one, zero).astype(HOT)
        tally = lax.dot_general(
            row_hot, low_hot, (((1,), (1,)), ((), ())), preferred_element_type=jnp.float32
        ).astype(jnp.bfloat16)
        base = pl.multiple_of(unit * rows, rows)
        for top in range(tops):
            tally_ref[pl.ds(base, rows), top * LANES : (top + 1) * LANES] = tally[
                top * rows : (top + 1) * rows
            ]
        return 0

    chunks = out_sems.shape[0]
    span = units // chunks
    stores = []
    for chunk in range(chunks):
        lax.fori_loop(chunk * span, (chunk + 1) * span, unit_step, 0, unroll=4)
        part = pl.ds(chunk * span * rows, span * rows)
        begin = 0
        for spot, tally_hbm in enumerate(tally_hbms):
            size = tally_hbm.shape[1]
            store = pltpu.make_async_copy(
                tally_ref.at[part, pl.ds(begin, size)],
                tally_hbm.at[part],
                out_sems.at[chunk, spot],
            )
            store.start()
            stores.append(store)
            begin += size
    for load in loads[4:]:
        load.wait()
    grouped_ref[...] = jnp.dot(
        tally_ref[...], pressure_ref[...], preferred_element_type=jnp.float32
    )
    core = core_ref[0]
    share = mine_ref.shape[1]
    for part in range(UNIT):
        sums = [None] * (places + 1)
        for place in range(places):
            first = part * combos + place * kinds
            picked = [
                grouped_ref[pl.ds(first + kind, units, stride=rows), :] for kind in range(kinds)
            ]
            wide = jnp.concatenate(
                [
                    jnp.concatenate([g[:, w * voxels : (w + 1) * voxels] for g in picked], axis=1)
                    for w in range(2)
                ],
                axis=0,
            )
            taps = jnp.dot(
                jnp.concatenate(split_parts(wide, 3), axis=0),
                kernel_ref[...],
                preferred_element_type=jnp.float32,
            )
            count = 2 * units
            taps = taps[:count] + (taps[count : 2 * count] + taps[2 * count :])
            for half in range(2):
                piece = taps[:, half * frame : (half + 1) * frame]
                spot = place + half
                sums[spot] = piece if sums[spot] is None else sums[spot] + piece
        total = jnp.concatenate(sums, axis=1)
        total = jnp.concatenate([total[:units], total[units:]], axis=1)
        pairs = units // (2 * share)
        for pair in range(pairs):
            even = total[2 * pair * share : (2 * pair + 1) * share]
            odd = total[(2 * pair + 1) * share : (2 * pair + 2) * share]
            mine_ref[part * pairs + pair] = jnp.where(core == 0, even, odd)
            other_ref[part * pairs + pair] = jnp.where(core == 0, odd, even)
    for store in stores:
        store.wait()


def forward(blocks, frames, classes, counts, pressure, kern_rows, kinds, places, time_len):
    slots, sensors = blocks.shape
    combos = kinds * places
    block_count = pressure.shape[0]
    slabs = lax.axis_size("slab")
    core = (lax.axis_index("slab") % 2).reshape(1)
    anywhere = pl.BlockSpec(memory_space=pltpu.HBM)
    vmem = pl.BlockSpec(memory_space=pltpu.VMEM)
    half = (slabs // 2, sensors // slabs, 2 * time_len)
    tallies = [
        jax.ShapeDtypeStruct((sensors * combos, block_count * cuts // sum(SPANS)), jnp.bfloat16)
        for cuts in SPANS
    ]
    operands = (blocks, frames, classes, counts, pressure, kern_rows)
    *tallies, mine, other = pl.pallas_call(
        functools.partial(forward_kernel, kinds, places),
        in_specs=[pl.BlockSpec(memory_space=pltpu.SMEM)] + [anywhere] * 6,
        out_specs=[anywhere] * len(SPANS) + [vmem, vmem],
        out_shape=tallies
        + [
            jax.ShapeDtypeStruct(half, jnp.float32),
            jax.ShapeDtypeStruct(half, jnp.float32),
        ],
        scratch_shapes=[pltpu.VMEM(operand.shape, operand.dtype) for operand in operands]
        + [
            pltpu.VMEM((sensors * combos, block_count), jnp.bfloat16),
            pltpu.VMEM((sensors // UNIT, UNIT * slots), jnp.int32),
            pltpu.VMEM((sensors * combos, pressure.shape[1]), jnp.float32),
            pltpu.SemaphoreType.DMA((len(operands),)),
            pltpu.SemaphoreType.DMA((8, len(SPANS))),
        ],
        compiler_params=pltpu.CompilerParams(vmem_limit_bytes=48 << 20),
        name="forward",
    )(core, *[in_hbm(operand) for operand in operands])
    return tallies, mine, other


def fill_responses(kinds, places, order_ref, piece_refs, kernel_ref, resp_ref, back_ref, wide_ref):
    combos = kinds * places
    rows = UNIT * combos
    share = piece_refs[0].shape[0]
    sensors = back_ref.shape[0]
    units = sensors // UNIT
    time_len = back_ref.shape[1] // 2
    taps = kernel_ref.shape[1]
    frame = taps // 2
    width = wide_ref.shape[1]
    voxels = width // 2
    for spot, piece_ref in enumerate(piece_refs):
        start = pl.multiple_of(order_ref[spot] * share, share)
        back_ref[pl.ds(start, share), :] = piece_ref[...]
    for place in range(places):
        waves = []
        for w in range(2):
            start = w * time_len + place * frame
            waves.append(
                lax.dot_general(
                    back_ref[:, start : start + taps],
                    kernel_ref[...],
                    (((1,), (1,)), ((), ())),
                    preferred_element_type=jnp.float32,
                )
            )
        for kind in range(kinds):
            cut = slice(kind * voxels, (kind + 1) * voxels)
            both = jnp.concatenate([waves[0][:, cut], waves[1][:, cut]], axis=1)
            for part in range(UNIT):
                first = part * combos + place * kinds + kind
                wide_ref[pl.ds(first, units, stride=rows), :] = both[
                    part * units : (part + 1) * units
                ]
    high, low = split_parts(wide_ref[...].T, 2)
    resp_ref[:width] = high
    resp_ref[width:] = low


def backward_kernel(kinds, places, pieces, own_ref, tally_hbm, *refs):
    if pieces:
        order_ref, *piece_refs = refs[: pieces + 1]
        kernel_ref, resp_ref, kept_ref, *code_refs = refs[pieces + 1 : -5]
        tally_ref, grad_ref, sems, back_ref, wide_ref = refs[-5:]
    else:
        tally_ref = tally_hbm
        resp_ref, kept_ref, *code_refs, grad_ref = refs
    groups, share, span = grad_ref.shape
    loads = [None]
    if pieces:
        cuts = sems.shape[0]
        loads = []
        for cut in range(cuts):
            here = pl.ds(cut * (span // cuts), span // cuts)
            loads.append(
                pltpu.make_async_copy(tally_hbm.at[:, here], tally_ref.at[:, here], sems.at[cut])
            )
            loads[-1].start()
    if pieces:
        fill_responses(
            kinds, places, order_ref, piece_refs, kernel_ref, resp_ref, back_ref, wide_ref
        )
    width = groups * share
    for cut, load in enumerate(loads):
        if load is not None:
            load.wait()
        here = slice(cut * (span // len(loads)), (cut + 1) * (span // len(loads)))
        both = jnp.dot(resp_ref[...], tally_ref[:, here], preferred_element_type=jnp.float32)
        both = both[:width] + both[width:]
        for group in range(groups):
            grad_ref[group, :, here] = both[group * share : (group + 1) * share]
    own = own_ref[0]
    kept_ref[...] = grad_ref[own]
    lanes = code_refs[0].shape[1] - span
    lane = lax.broadcasted_iota(jnp.int32, (share, lanes), 1)
    for step, code_ref in enumerate(code_refs, 1):
        levels = jnp.zeros((share, lanes), jnp.int32)
        for spot in range(span // GRAIN):
            cut = slice(spot * GRAIN, (spot + 1) * GRAIN)
            block = grad_ref[own ^ step, :, cut]
            top = jnp.maximum(jnp.max(jnp.abs(block), axis=1, keepdims=True), TINY)
            level = jnp.minimum(jnp.floor(jnp.log(top) * RATE) + 2.0, CODE)
            code = block * jnp.exp(level * (-1.0 / RATE)) * CODE
            code_ref[:, cut] = jnp.floor(code + 0.5).astype(jnp.int32).astype(jnp.int16)
            levels = jnp.where(lane == spot, level.astype(jnp.int32), levels)
        code_ref[:, span:] = levels.astype(jnp.int16)


def backward(own, tally, width, resp=None, order=None, pieces=(), kern_rows=None, combos=None):
    groups = lax.axis_size("sens")
    share, (rows, span) = width // groups, tally.shape
    vmem = pl.BlockSpec(memory_space=pltpu.VMEM)
    smem = pl.BlockSpec(memory_space=pltpu.SMEM)
    hbm = pl.BlockSpec(memory_space=pltpu.HBM)
    out_shape = [jax.ShapeDtypeStruct((share, span), jnp.float32)] + [
        jax.ShapeDtypeStruct((share, span + 128), jnp.int16)
    ] * (groups - 1)
    scratch = [pltpu.VMEM((groups, share, span), jnp.float32)]
    if resp is None:
        tally = in_hbm(tally)
        scratch = [
            pltpu.VMEM((rows, span), tally.dtype),
            *scratch,
            pltpu.SemaphoreType.DMA((span // CUT,)),
        ]
        operands = (order, *pieces, pltpu.with_memory_space_constraint(kern_rows, pltpu.VMEM))
        specs = [smem] + [vmem] * (len(pieces) + 1)
        out_shape = [jax.ShapeDtypeStruct((2 * width, rows), jnp.bfloat16)] + out_shape
        length = pieces[0].shape[1]
        sensors = pieces[0].shape[0] * len(pieces)
        scratch += [
            pltpu.VMEM((sensors, length), jnp.bfloat16),
            pltpu.VMEM((rows, width), jnp.float32),
        ]
    else:
        tally, hbm = pltpu.with_memory_space_constraint(tally, pltpu.VMEM), vmem
        operands, specs = (resp,), [vmem]
    outs = pl.pallas_call(
        functools.partial(backward_kernel, *(combos or (0, 0)), len(pieces)),
        in_specs=[smem, hbm] + specs,
        out_specs=[vmem] * len(out_shape),
        out_shape=out_shape,
        scratch_shapes=scratch,
        compiler_params=pltpu.CompilerParams(vmem_limit_bytes=24 << 20),
        cost_estimate=pl.CostEstimate(
            flops=4 * width * rows * span * 1, bytes_accessed=2 * rows * span, transcendentals=0
        ),
        name="backward",
    )(own, tally, *operands)
    if resp is None:
        resp, *outs = outs
    kept, *codes = outs
    received = []
    for step in range(groups - 1, 0, -1):
        pairs = [(q, q ^ step) for q in range(groups)]
        received.append(lax.ppermute(codes[step - 1], "sens", pairs))
    return resp, [kept, *received]


def finish_kernel(*refs):
    part_refs, out_ref = refs[:-1], refs[-1]
    count = len(part_refs) // len(SPANS)
    begin = 0
    for part in range(len(SPANS)):
        kept_ref, *code_refs = part_refs[part * count : (part + 1) * count]
        span = kept_ref.shape[1]
        for spot in range(span // GRAIN):
            cut = slice(spot * GRAIN, (spot + 1) * GRAIN)
            total = kept_ref[:, cut]
            for code_ref in code_refs:
                level = code_ref[:, span:].astype(jnp.int32).astype(jnp.float32)[:, spot : spot + 1]
                scale = jnp.exp(level * (1.0 / RATE)) * (1.0 / CODE)
                total = total + code_ref[:, cut].astype(jnp.int32).astype(jnp.float32) * scale
            out_ref[:, begin : begin + GRAIN] = total
            begin += GRAIN


def finish(parts, block_count):
    return pl.pallas_call(
        finish_kernel,
        out_shape=jax.ShapeDtypeStruct((parts[0].shape[0], block_count), jnp.float32),
        compiler_params=pltpu.CompilerParams(vmem_limit_bytes=8 << 20),
        name="finish",
    )(*parts)


def scatter_slab(mine, other, gains):
    slabs = lax.axis_size("slab")
    chips = slabs // 2
    place = lax.axis_index("slab")
    chip = place // 2
    paired = mine + lax.ppermute(other, "slab", [(j, j ^ 1) for j in range(slabs)])
    paired, gains = lax.optimization_barrier((paired, gains))
    received = [lax.dynamic_index_in_dim(paired, chip, 0, keepdims=False)]
    for step in (2, 1, 3) if chips == 4 else range(1, chips):
        block = lax.dynamic_index_in_dim(paired, chip ^ step, 0, keepdims=False)
        received.append(
            lax.ppermute(block, "slab", [(j, j ^ (2 * step)) for j in range(slabs)])
        )
    return received, gains


def refine_kernel(*refs):
    *piece_refs, matrix_ref, measured_ref, residual_ref, back_ref = refs
    total = piece_refs[0][...]
    for piece_ref in piece_refs[1:]:
        total = total + piece_ref[...]
    share, length = total.shape
    half = length // 2
    rows = jnp.concatenate([total[:, :half], total[:, half:]], axis=0)
    dot = functools.partial(
        jnp.dot, precision=lax.Precision.HIGHEST, preferred_element_type=jnp.float32
    )
    residual = dot(rows, matrix_ref[...]) - measured_ref[...]
    residual_ref[...] = residual
    back = dot(residual, matrix_ref[...]).astype(jnp.bfloat16)
    back_ref[:, :half] = back[:share]
    back_ref[:, half:] = back[share:]


def refine(received, matrix, measured):
    share, length = received[0].shape
    return pl.pallas_call(
        refine_kernel,
        out_shape=[
            jax.ShapeDtypeStruct(measured.shape, jnp.float32),
            jax.ShapeDtypeStruct((share, length), jnp.bfloat16),
        ],
        compiler_params=pltpu.CompilerParams(vmem_limit_bytes=12 << 20),
        name="refine",
    )(*[pltpu.with_memory_space_constraint(piece, pltpu.VMEM) for piece in received], matrix, measured)


def gather_slab(share):
    slabs = lax.axis_size("slab")
    place = lax.axis_index("slab")
    pieces, order = [share], [place]
    for step in range(slabs // 2 - 1, 0, -1):
        pieces.append(lax.ppermute(share, "slab", [(j, j ^ (2 * step)) for j in range(slabs)]))
        order.append(place ^ (2 * step))
    for spot in range(slabs // 2):
        pieces.append(lax.ppermute(pieces[spot], "slab", [(j, j ^ 1) for j in range(slabs)]))
        order.append(order[spot] ^ 1)
    return pieces, jnp.stack(order).astype(jnp.int32)


def per_device(pressure, kernels, filter_gains, measured, blocks, frames, classes, counts):
    kinds, voxels, taps = kernels.shape
    block_count, width = pressure.shape
    frame = taps // 2
    time_len = filter_gains.shape[0]
    places = time_len // frame - 1
    combos = kinds * places
    sensors, slots = blocks.shape[0], blocks.shape[2]
    share = sensors // lax.axis_size("slab")

    kern_rows = kernels.reshape(kinds * voxels, taps)

    tallies, mine, other = forward(
        blocks[:, 0, :].T,
        frames[:, 0, :].T,
        classes[:, 0, :].T,
        counts.T,
        pressure,
        kern_rows,
        kinds,
        places,
        time_len,
    )
    received, gains = scatter_slab(mine, other, filter_gains)
    matrix, kern_fast = filter_matrix(gains, kern_rows)
    measured_share = lax.dynamic_slice_in_dim(measured, lax.axis_index("slab") * share, share, 0)
    measured_share = measured_share.transpose(1, 0, 2).reshape(2 * share, time_len)
    residual, back = refine(received, matrix, measured_share)
    residual = residual.reshape(2, share, time_len).transpose(1, 0, 2)
    pieces, order = gather_slab(back)
    own = lax.axis_index("sens").reshape(1)
    resp, parts = backward(
        own, tallies[0], width, None, order, pieces, kern_fast, (kinds, places)
    )
    parts = parts + backward(own, tallies[1], width, resp)[1]
    gradient = finish(parts, block_count).T
    return (residual, gradient)


def solution(mesh):
    return jax.shard_map(
        per_device,
        mesh=mesh,
        in_specs=(
            P("slab", None),
            P(),
            P(),
            P("sens", None, None),
            P("sens", "slab", None),
            P("sens", "slab", None),
            P("sens", "slab", None),
            P("sens", "slab"),
        ),
        out_specs=(P(("sens", "slab"), None, None), P("slab", "sens")),
        check_vma=False,
    )
```

```python
import functools
import math

import jax
import jax.numpy as jnp
import numpy as np
from jax import lax
from jax.experimental import pallas as pl
from jax.experimental.pallas import tpu as pltpu
from jax.sharding import PartitionSpec as P

LANES = 256
UNIT = 4
HOT = jnp.float8_e4m3fn
CODE = 32766.0
TINY = 1e-37
RATE = 256 / math.log(2.0)
GRAIN = 256
SPANS = (4, 4)
CUT = 512


def in_hbm(array):
    return pltpu.with_memory_space_constraint(array, pltpu.HBM)


def to_bf16(array):
    return array.astype(jnp.float32).astype(jnp.bfloat16)


def filter_kernel(gains_hbm, cosine_hbm, kernel_hbm, matrix_ref, fast_ref, *refs):
    gains_ref, cosine_ref, sems = refs
    pairs = [(gains_hbm, gains_ref), (cosine_hbm, cosine_ref), (kernel_hbm, fast_ref)]
    copies = [
        pltpu.make_async_copy(source, target, sems.at[spot])
        for spot, (source, target) in enumerate(pairs)
    ]
    for copy in copies:
        copy.start()
    for copy in copies[:2]:
        copy.wait()
    time_len = cosine_ref.shape[0]
    row = jnp.dot(
        jnp.broadcast_to(gains_ref[...], (8, time_len)),
        cosine_ref[...],
        precision=lax.Precision.HIGHEST,
        preferred_element_type=jnp.float32,
    )
    wide = jnp.broadcast_to(row[:1] / time_len, (time_len, time_len))
    matrix_ref[...] = pltpu.roll(wide, 0, axis=1, stride=1, stride_axis=0)
    for copy in copies[2:]:
        copy.wait()


def filter_matrix(filter_gains, kern_rows):
    time_len = filter_gains.shape[0]
    ids = np.arange(time_len)
    cosine = np.cos(np.outer(ids, ids) % time_len * (2.0 * math.pi / time_len))
    operands = (filter_gains[None, :], jnp.asarray(cosine, jnp.float32), kern_rows)
    return pl.pallas_call(
        filter_kernel,
        in_specs=[pl.BlockSpec(memory_space=pltpu.HBM)] * 3,
        out_specs=[pl.BlockSpec(memory_space=pltpu.VMEM)] * 2,
        out_shape=[
            pltpu.VMEM((time_len, time_len), jnp.float32),
            pltpu.VMEM(kern_rows.shape, kern_rows.dtype),
        ],
        scratch_shapes=[
            pltpu.VMEM((1, time_len), jnp.float32),
            pltpu.VMEM((time_len, time_len), jnp.float32),
            pltpu.SemaphoreType.DMA((3,)),
        ],
        compiler_params=pltpu.CompilerParams(vmem_limit_bytes=8 << 20),
        name="filter_matrix",
    )(*[in_hbm(operand) for operand in operands])


def split_parts(array, count):
    parts = []
    for _ in range(count):
        part = array.astype(jnp.bfloat16)
        parts.append(part)
        array = array - part.astype(jnp.float32)
    return parts


def forward_kernel(
    kinds,
    places,
    core_ref,
    blocks_hbm,
    frames_hbm,
    classes_hbm,
    counts_hbm,
    pressure_hbm,
    kernel_hbm,
    *refs,
):
    tally_hbms = refs[: len(SPANS)]
    (
        mine_ref,
        other_ref,
        blocks_ref,
        frames_ref,
        classes_ref,
        counts_ref,
        pressure_ref,
        kernel_ref,
        tally_ref,
        code_ref,
        grouped_ref,
        in_sems,
        out_sems,
    ) = refs[len(SPANS) :]
    loads = [
        pltpu.make_async_copy(source, target, in_sems.at[spot])
        for spot, (source, target) in enumerate(
            (
                (blocks_hbm, blocks_ref),
                (frames_hbm, frames_ref),
                (classes_hbm, classes_ref),
                (counts_hbm, counts_ref),
                (pressure_hbm, pressure_ref),
                (kernel_hbm, kernel_ref),
            )
        )
    ]
    for load in loads:
        load.start()
    for load in loads[:4]:
        load.wait()
    combos = kinds * places
    rows = UNIT * combos
    block_count = pressure_ref.shape[0]
    tops = block_count // LANES
    slots, sensors = blocks_ref.shape
    units = sensors // UNIT
    voxels = pressure_ref.shape[1] // 2
    frame = kernel_ref.shape[1] // 2

    block_ids = blocks_ref[...]
    lane = lax.broadcasted_iota(jnp.int32, (slots, sensors), 1) // units
    row_ids = lane * combos + frames_ref[...] * kinds + classes_ref[...]
    live = lax.broadcasted_iota(jnp.int32, (slots, sensors), 0) < counts_ref[...]
    code = jnp.where(live, row_ids * block_count + block_ids, -1).T
    code_ref[...] = jnp.concatenate(
        [code[part * units : (part + 1) * units] for part in range(UNIT)], axis=1
    )

    width = UNIT * slots
    step = 16
    row_iota = to_bf16(lax.broadcasted_iota(jnp.int32, (rows, width), 0))
    low_iota = to_bf16(lax.broadcasted_iota(jnp.int32, (LANES, width), 0))
    one, zero = jnp.ones((), jnp.bfloat16), jnp.zeros((), jnp.bfloat16)
    shift = LANES.bit_length() - 1
    depth = block_count.bit_length() - 1

    def unit_step(unit, _):
        code = code_ref[pl.ds(unit, 1), :]
        row_code = to_bf16(lax.shift_right_arithmetic(code, depth))
        top_code = to_bf16(lax.shift_right_arithmetic(code & (block_count - 1), shift))
        low_code = to_bf16(code & (LANES - 1))
        picked = jnp.where(row_iota == row_code, one, zero)
        top_code = jnp.broadcast_to(top_code, (step, width))
        row_hot = []
        for top in range(tops):
            here = top_code == jnp.bfloat16(top)
            for cut in range(0, rows, step):
                row_hot.append(jnp.where(here, picked[cut : cut + step], zero))
        row_hot = jnp.concatenate(row_hot, axis=0).astype(HOT)
        low_hot = jnp.where(low_iota == low_code, one, zero).astype(HOT)
        tally = lax.dot_general(
            row_hot, low_hot, (((1,), (1,)), ((), ())), preferred_element_type=jnp.float32
        ).astype(jnp.bfloat16)
        base = pl.multiple_of(unit * rows, rows)
        for top in range(tops):
            tally_ref[pl.ds(base, rows), top * LANES : (top + 1) * LANES] = tally[
                top * rows : (top + 1) * rows
            ]
        return 0

    chunks = out_sems.shape[0]
    span = units // chunks
    stores = []
    for chunk in range(chunks):
        lax.fori_loop(chunk * span, (chunk + 1) * span, unit_step, 0, unroll=8)
        part = pl.ds(chunk * span * rows, span * rows)
        begin = 0
        for spot, tally_hbm in enumerate(tally_hbms):
            size = tally_hbm.shape[1]
            store = pltpu.make_async_copy(
                tally_ref.at[part, pl.ds(begin, size)],
                tally_hbm.at[part],
                out_sems.at[chunk, spot],
            )
            store.start()
            stores.append(store)
            begin += size
    for load in loads[4:]:
        load.wait()
    grouped_ref[...] = jnp.dot(
        tally_ref[...], pressure_ref[...], preferred_element_type=jnp.float32
    )
    core = core_ref[0]
    share = mine_ref.shape[1]
    for part in range(UNIT):
        sums = [None] * (places + 1)
        for place in range(places):
            first = part * combos + place * kinds
            picked = [
                grouped_ref[pl.ds(first + kind, units, stride=rows), :] for kind in range(kinds)
            ]
            wide = jnp.concatenate(
                [
                    jnp.concatenate([g[:, w * voxels : (w + 1) * voxels] for g in picked], axis=1)
                    for w in range(2)
                ],
                axis=0,
            )
            taps = jnp.dot(
                jnp.concatenate(split_parts(wide, 3), axis=0),
                kernel_ref[...],
                preferred_element_type=jnp.float32,
            )
            count = 2 * units
            taps = taps[:count] + (taps[count : 2 * count] + taps[2 * count :])
            for half in range(2):
                piece = taps[:, half * frame : (half + 1) * frame]
                spot = place + half
                sums[spot] = piece if sums[spot] is None else sums[spot] + piece
        total = jnp.concatenate(sums, axis=1)
        total = jnp.concatenate([total[:units], total[units:]], axis=1)
        pairs = units // (2 * share)
        for pair in range(pairs):
            even = total[2 * pair * share : (2 * pair + 1) * share]
            odd = total[(2 * pair + 1) * share : (2 * pair + 2) * share]
            mine_ref[part * pairs + pair] = jnp.where(core == 0, even, odd)
            other_ref[part * pairs + pair] = jnp.where(core == 0, odd, even)
    for store in stores:
        store.wait()


def forward(blocks, frames, classes, counts, pressure, kern_rows, kinds, places, time_len):
    slots, sensors = blocks.shape
    combos = kinds * places
    block_count = pressure.shape[0]
    slabs = lax.axis_size("slab")
    core = (lax.axis_index("slab") % 2).reshape(1)
    anywhere = pl.BlockSpec(memory_space=pltpu.HBM)
    vmem = pl.BlockSpec(memory_space=pltpu.VMEM)
    half = (slabs // 2, sensors // slabs, 2 * time_len)
    tallies = [
        jax.ShapeDtypeStruct((sensors * combos, block_count * cuts // sum(SPANS)), jnp.bfloat16)
        for cuts in SPANS
    ]
    operands = (blocks, frames, classes, counts, pressure, kern_rows)
    *tallies, mine, other = pl.pallas_call(
        functools.partial(forward_kernel, kinds, places),
        in_specs=[pl.BlockSpec(memory_space=pltpu.SMEM)] + [anywhere] * 6,
        out_specs=[anywhere] * len(SPANS) + [vmem, vmem],
        out_shape=tallies
        + [
            jax.ShapeDtypeStruct(half, jnp.float32),
            jax.ShapeDtypeStruct(half, jnp.float32),
        ],
        scratch_shapes=[pltpu.VMEM(operand.shape, operand.dtype) for operand in operands]
        + [
            pltpu.VMEM((sensors * combos, block_count), jnp.bfloat16),
            pltpu.VMEM((sensors // UNIT, UNIT * slots), jnp.int32),
            pltpu.VMEM((sensors * combos, pressure.shape[1]), jnp.float32),
            pltpu.SemaphoreType.DMA((len(operands),)),
            pltpu.SemaphoreType.DMA((4, len(SPANS))),
        ],
        compiler_params=pltpu.CompilerParams(vmem_limit_bytes=48 << 20),
        name="forward",
    )(core, *[in_hbm(operand) for operand in operands])
    return tallies, mine, other


def fill_responses(kinds, places, order_ref, piece_refs, kernel_ref, resp_ref, back_ref, wide_ref):
    combos = kinds * places
    rows = UNIT * combos
    share = piece_refs[0].shape[0]
    sensors = back_ref.shape[0]
    units = sensors // UNIT
    time_len = back_ref.shape[1] // 2
    taps = kernel_ref.shape[1]
    frame = taps // 2
    width = wide_ref.shape[1]
    voxels = width // 2
    for spot, piece_ref in enumerate(piece_refs):
        start = pl.multiple_of(order_ref[spot] * share, share)
        back_ref[pl.ds(start, share), :] = piece_ref[...]
    for place in range(places):
        waves = []
        for w in range(2):
            start = w * time_len + place * frame
            waves.append(
                lax.dot_general(
                    back_ref[:, start : start + taps],
                    kernel_ref[...],
                    (((1,), (1,)), ((), ())),
                    preferred_element_type=jnp.float32,
                )
            )
        for kind in range(kinds):
            cut = slice(kind * voxels, (kind + 1) * voxels)
            both = jnp.concatenate([waves[0][:, cut], waves[1][:, cut]], axis=1)
            for part in range(UNIT):
                first = part * combos + place * kinds + kind
                wide_ref[pl.ds(first, units, stride=rows), :] = both[
                    part * units : (part + 1) * units
                ]
    high, low = split_parts(wide_ref[...].T, 2)
    resp_ref[:width] = high
    resp_ref[width:] = low


def backward_kernel(kinds, places, pieces, own_ref, tally_hbm, *refs):
    if pieces:
        order_ref, *piece_refs = refs[: pieces + 1]
        kernel_ref, resp_ref, kept_ref, *code_refs = refs[pieces + 1 : -5]
        tally_ref, grad_ref, sems, back_ref, wide_ref = refs[-5:]
    else:
        tally_ref = tally_hbm
        resp_ref, kept_ref, *code_refs, grad_ref = refs
    groups, share, span = grad_ref.shape
    loads = [None]
    if pieces:
        cuts = sems.shape[0]
        loads = []
        for cut in range(cuts):
            here = pl.ds(cut * (span // cuts), span // cuts)
            loads.append(
                pltpu.make_async_copy(tally_hbm.at[:, here], tally_ref.at[:, here], sems.at[cut])
            )
            loads[-1].start()
    if pieces:
        fill_responses(
            kinds, places, order_ref, piece_refs, kernel_ref, resp_ref, back_ref, wide_ref
        )
    width = groups * share
    for cut, load in enumerate(loads):
        if load is not None:
            load.wait()
        here = slice(cut * (span // len(loads)), (cut + 1) * (span // len(loads)))
        both = jnp.dot(resp_ref[...], tally_ref[:, here], preferred_element_type=jnp.float32)
        both = both[:width] + both[width:]
        for group in range(groups):
            grad_ref[group, :, here] = both[group * share : (group + 1) * share]
    own = own_ref[0]
    kept_ref[...] = grad_ref[own]
    lanes = code_refs[0].shape[1] - span
    lane = lax.broadcasted_iota(jnp.int32, (share, lanes), 1)
    for step, code_ref in enumerate(code_refs, 1):
        levels = jnp.zeros((share, lanes), jnp.int32)
        for spot in range(span // GRAIN):
            cut = slice(spot * GRAIN, (spot + 1) * GRAIN)
            block = grad_ref[own ^ step, :, cut]
            top = jnp.maximum(jnp.max(jnp.abs(block), axis=1, keepdims=True), TINY)
            level = jnp.minimum(jnp.floor(jnp.log(top) * RATE) + 2.0, CODE)
            code = block * jnp.exp(level * (-1.0 / RATE)) * CODE
            code_ref[:, cut] = jnp.floor(code + 0.5).astype(jnp.int32).astype(jnp.int16)
            levels = jnp.where(lane == spot, level.astype(jnp.int32), levels)
        code_ref[:, span:] = levels.astype(jnp.int16)


def backward(own, tally, width, resp=None, order=None, pieces=(), kern_rows=None, combos=None):
    groups = lax.axis_size("sens")
    share, (rows, span) = width // groups, tally.shape
    vmem = pl.BlockSpec(memory_space=pltpu.VMEM)
    smem = pl.BlockSpec(memory_space=pltpu.SMEM)
    hbm = pl.BlockSpec(memory_space=pltpu.HBM)
    out_shape = [jax.ShapeDtypeStruct((share, span), jnp.float32)] + [
        jax.ShapeDtypeStruct((share, span + 128), jnp.int16)
    ] * (groups - 1)
    scratch = [pltpu.VMEM((groups, share, span), jnp.float32)]
    if resp is None:
        tally = in_hbm(tally)
        scratch = [
            pltpu.VMEM((rows, span), tally.dtype),
            *scratch,
            pltpu.SemaphoreType.DMA((span // CUT,)),
        ]
        operands = (order, *pieces, pltpu.with_memory_space_constraint(kern_rows, pltpu.VMEM))
        specs = [smem] + [vmem] * (len(pieces) + 1)
        out_shape = [jax.ShapeDtypeStruct((2 * width, rows), jnp.bfloat16)] + out_shape
        length = pieces[0].shape[1]
        sensors = pieces[0].shape[0] * len(pieces)
        scratch += [
            pltpu.VMEM((sensors, length), jnp.bfloat16),
            pltpu.VMEM((rows, width), jnp.float32),
        ]
    else:
        tally, hbm = pltpu.with_memory_space_constraint(tally, pltpu.VMEM), vmem
        operands, specs = (resp,), [vmem]
    outs = pl.pallas_call(
        functools.partial(backward_kernel, *(combos or (0, 0)), len(pieces)),
        in_specs=[smem, hbm] + specs,
        out_specs=[vmem] * len(out_shape),
        out_shape=out_shape,
        scratch_shapes=scratch,
        compiler_params=pltpu.CompilerParams(vmem_limit_bytes=24 << 20),
        cost_estimate=pl.CostEstimate(
            flops=4 * width * rows * span * 1, bytes_accessed=2 * rows * span, transcendentals=0
        ),
        name="backward",
    )(own, tally, *operands)
    if resp is None:
        resp, *outs = outs
    kept, *codes = outs
    received = []
    for step in range(groups - 1, 0, -1):
        pairs = [(q, q ^ step) for q in range(groups)]
        received.append(lax.ppermute(codes[step - 1], "sens", pairs))
    return resp, [kept, *received]


def finish_kernel(*refs):
    part_refs, out_ref = refs[:-1], refs[-1]
    count = len(part_refs) // len(SPANS)
    begin = 0
    for part in range(len(SPANS)):
        kept_ref, *code_refs = part_refs[part * count : (part + 1) * count]
        span = kept_ref.shape[1]
        for spot in range(span // GRAIN):
            cut = slice(spot * GRAIN, (spot + 1) * GRAIN)
            total = kept_ref[:, cut]
            for code_ref in code_refs:
                level = code_ref[:, span:].astype(jnp.int32).astype(jnp.float32)[:, spot : spot + 1]
                scale = jnp.exp(level * (1.0 / RATE)) * (1.0 / CODE)
                total = total + code_ref[:, cut].astype(jnp.int32).astype(jnp.float32) * scale
            out_ref[:, begin : begin + GRAIN] = total
            begin += GRAIN


def finish(parts, block_count):
    return pl.pallas_call(
        finish_kernel,
        out_shape=jax.ShapeDtypeStruct((parts[0].shape[0], block_count), jnp.float32),
        compiler_params=pltpu.CompilerParams(vmem_limit_bytes=8 << 20),
        name="finish",
    )(*parts)


def scatter_slab(mine, other, gains):
    slabs = lax.axis_size("slab")
    chips = slabs // 2
    place = lax.axis_index("slab")
    chip = place // 2
    paired = mine + lax.ppermute(other, "slab", [(j, j ^ 1) for j in range(slabs)])
    paired, gains = lax.optimization_barrier((paired, gains))
    received = [lax.dynamic_index_in_dim(paired, chip, 0, keepdims=False)]
    for step in (2, 1, 3) if chips == 4 else range(1, chips):
        block = lax.dynamic_index_in_dim(paired, chip ^ step, 0, keepdims=False)
        received.append(
            lax.ppermute(block, "slab", [(j, j ^ (2 * step)) for j in range(slabs)])
        )
    return received, gains


def refine_kernel(*refs):
    *piece_refs, matrix_ref, measured_ref, residual_ref, back_ref = refs
    total = piece_refs[0][...]
    for piece_ref in piece_refs[1:]:
        total = total + piece_ref[...]
    share, length = total.shape
    half = length // 2
    rows = jnp.concatenate([total[:, :half], total[:, half:]], axis=0)
    dot = functools.partial(
        jnp.dot, precision=lax.Precision.HIGHEST, preferred_element_type=jnp.float32
    )
    residual = dot(rows, matrix_ref[...]) - measured_ref[...]
    residual_ref[...] = residual
    back = dot(residual, matrix_ref[...]).astype(jnp.bfloat16)
    back_ref[:, :half] = back[:share]
    back_ref[:, half:] = back[share:]


def refine(received, matrix, measured):
    share, length = received[0].shape
    return pl.pallas_call(
        refine_kernel,
        out_shape=[
            jax.ShapeDtypeStruct(measured.shape, jnp.float32),
            jax.ShapeDtypeStruct((share, length), jnp.bfloat16),
        ],
        compiler_params=pltpu.CompilerParams(vmem_limit_bytes=12 << 20),
        name="refine",
    )(*[pltpu.with_memory_space_constraint(piece, pltpu.VMEM) for piece in received], matrix, measured)


def gather_slab(share):
    slabs = lax.axis_size("slab")
    place = lax.axis_index("slab")
    pieces, order = [share], [place]
    for step in range(slabs // 2 - 1, 0, -1):
        pieces.append(lax.ppermute(share, "slab", [(j, j ^ (2 * step)) for j in range(slabs)]))
        order.append(place ^ (2 * step))
    for spot in range(slabs // 2):
        pieces.append(lax.ppermute(pieces[spot], "slab", [(j, j ^ 1) for j in range(slabs)]))
        order.append(order[spot] ^ 1)
    return pieces, jnp.stack(order).astype(jnp.int32)


def per_device(pressure, kernels, filter_gains, measured, blocks, frames, classes, counts):
    kinds, voxels, taps = kernels.shape
    block_count, width = pressure.shape
    frame = taps // 2
    time_len = filter_gains.shape[0]
    places = time_len // frame - 1
    combos = kinds * places
    sensors, slots = blocks.shape[0], blocks.shape[2]
    share = sensors // lax.axis_size("slab")

    kern_rows = kernels.reshape(kinds * voxels, taps)

    tallies, mine, other = forward(
        blocks[:, 0, :].T,
        frames[:, 0, :].T,
        classes[:, 0, :].T,
        counts.T,
        pressure,
        kern_rows,
        kinds,
        places,
        time_len,
    )
    received, gains = scatter_slab(mine, other, filter_gains)
    matrix, kern_fast = filter_matrix(gains, kern_rows)
    measured_share = lax.dynamic_slice_in_dim(measured, lax.axis_index("slab") * share, share, 0)
    measured_share = measured_share.transpose(1, 0, 2).reshape(2 * share, time_len)
    residual, back = refine(received, matrix, measured_share)
    residual = residual.reshape(2, share, time_len).transpose(1, 0, 2)
    pieces, order = gather_slab(back)
    own = lax.axis_index("sens").reshape(1)
    resp, parts = backward(
        own, tallies[0], width, None, order, pieces, kern_fast, (kinds, places)
    )
    parts = parts + backward(own, tallies[1], width, resp)[1]
    gradient = finish(parts, block_count).T
    return (residual, gradient)


def solution(mesh):
    return jax.shard_map(
        per_device,
        mesh=mesh,
        in_specs=(
            P("slab", None),
            P(),
            P(),
            P("sens", None, None),
            P("sens", "slab", None),
            P("sens", "slab", None),
            P("sens", "slab", None),
            P("sens", "slab"),
        ),
        out_specs=(P(("sens", "slab"), None, None), P("slab", "sens")),
        check_vma=False,
    )
```

```python
import functools
import math

import jax
import jax.numpy as jnp
import numpy as np
from jax import lax
from jax.experimental import pallas as pl
from jax.experimental.pallas import tpu as pltpu
from jax.sharding import PartitionSpec as P

LANES = 256
UNIT = 4
HOT = jnp.float8_e4m3fn
CODE = 32766.0
TINY = 1e-37
RATE = 256 / math.log(2.0)
GRAIN = 512
SPANS = (4, 4)
CUT = 512


def in_hbm(array):
    return pltpu.with_memory_space_constraint(array, pltpu.HBM)


def to_bf16(array):
    return array.astype(jnp.float32).astype(jnp.bfloat16)


def filter_kernel(gains_hbm, cosine_hbm, kernel_hbm, matrix_ref, fast_ref, *refs):
    gains_ref, cosine_ref, sems = refs
    pairs = [(gains_hbm, gains_ref), (cosine_hbm, cosine_ref), (kernel_hbm, fast_ref)]
    copies = [
        pltpu.make_async_copy(source, target, sems.at[spot])
        for spot, (source, target) in enumerate(pairs)
    ]
    for copy in copies:
        copy.start()
    for copy in copies[:2]:
        copy.wait()
    time_len = cosine_ref.shape[0]
    row = jnp.dot(
        jnp.broadcast_to(gains_ref[...], (8, time_len)),
        cosine_ref[...],
        precision=lax.Precision.HIGHEST,
        preferred_element_type=jnp.float32,
    )
    wide = jnp.broadcast_to(row[:1] / time_len, (time_len, time_len))
    matrix_ref[...] = pltpu.roll(wide, 0, axis=1, stride=1, stride_axis=0)
    for copy in copies[2:]:
        copy.wait()


def filter_matrix(filter_gains, kern_rows):
    time_len = filter_gains.shape[0]
    ids = np.arange(time_len)
    cosine = np.cos(np.outer(ids, ids) % time_len * (2.0 * math.pi / time_len))
    operands = (filter_gains[None, :], jnp.asarray(cosine, jnp.float32), kern_rows)
    return pl.pallas_call(
        filter_kernel,
        in_specs=[pl.BlockSpec(memory_space=pltpu.HBM)] * 3,
        out_specs=[pl.BlockSpec(memory_space=pltpu.VMEM)] * 2,
        out_shape=[
            pltpu.VMEM((time_len, time_len), jnp.float32),
            pltpu.VMEM(kern_rows.shape, kern_rows.dtype),
        ],
        scratch_shapes=[
            pltpu.VMEM((1, time_len), jnp.float32),
            pltpu.VMEM((time_len, time_len), jnp.float32),
            pltpu.SemaphoreType.DMA((3,)),
        ],
        compiler_params=pltpu.CompilerParams(vmem_limit_bytes=8 << 20),
        name="filter_matrix",
    )(*[in_hbm(operand) for operand in operands])


def split_parts(array, count):
    parts = []
    for _ in range(count):
        part = array.astype(jnp.bfloat16)
        parts.append(part)
        array = array - part.astype(jnp.float32)
    return parts


def forward_kernel(
    kinds,
    places,
    core_ref,
    blocks_hbm,
    frames_hbm,
    classes_hbm,
    counts_hbm,
    pressure_hbm,
    kernel_hbm,
    *refs,
):
    tally_hbms = refs[: len(SPANS)]
    (
        mine_ref,
        other_ref,
        blocks_ref,
        frames_ref,
        classes_ref,
        counts_ref,
        pressure_ref,
        kernel_ref,
        tally_ref,
        code_ref,
        grouped_ref,
        in_sems,
        out_sems,
    ) = refs[len(SPANS) :]
    loads = [
        pltpu.make_async_copy(source, target, in_sems.at[spot])
        for spot, (source, target) in enumerate(
            (
                (blocks_hbm, blocks_ref),
                (frames_hbm, frames_ref),
                (classes_hbm, classes_ref),
                (counts_hbm, counts_ref),
                (pressure_hbm, pressure_ref),
                (kernel_hbm, kernel_ref),
            )
        )
    ]
    for load in loads:
        load.start()
    for load in loads[:4]:
        load.wait()
    combos = kinds * places
    rows = UNIT * combos
    block_count = pressure_ref.shape[0]
    tops = block_count // LANES
    slots, sensors = blocks_ref.shape
    units = sensors // UNIT
    voxels = pressure_ref.shape[1] // 2
    frame = kernel_ref.shape[1] // 2

    block_ids = blocks_ref[...]
    lane = lax.broadcasted_iota(jnp.int32, (slots, sensors), 1) // units
    row_ids = lane * combos + frames_ref[...] * kinds + classes_ref[...]
    live = lax.broadcasted_iota(jnp.int32, (slots, sensors), 0) < counts_ref[...]
    code = jnp.where(live, row_ids * block_count + block_ids, -1).T
    code_ref[...] = jnp.concatenate(
        [code[part * units : (part + 1) * units] for part in range(UNIT)], axis=1
    )

    width = UNIT * slots
    step = 16
    row_iota = to_bf16(lax.broadcasted_iota(jnp.int32, (rows, width), 0))
    low_iota = to_bf16(lax.broadcasted_iota(jnp.int32, (LANES, width), 0))
    one, zero = jnp.ones((), jnp.bfloat16), jnp.zeros((), jnp.bfloat16)
    shift = LANES.bit_length() - 1
    depth = block_count.bit_length() - 1

    def unit_step(unit, _):
        code = code_ref[pl.ds(unit, 1), :]
        row_code = to_bf16(lax.shift_right_arithmetic(code, depth))
        top_code = to_bf16(lax.shift_right_arithmetic(code & (block_count - 1), shift))
        low_code = to_bf16(code & (LANES - 1))
        picked = jnp.where(row_iota == row_code, one, zero)
        top_code = jnp.broadcast_to(top_code, (step, width))
        row_hot = []
        for top in range(tops):
            here = top_code == jnp.bfloat16(top)
            for cut in range(0, rows, step):
                row_hot.append(jnp.where(here, picked[cut : cut + step], zero))
        row_hot = jnp.concatenate(row_hot, axis=0).astype(HOT)
        low_hot = jnp.where(low_iota == low_code, one, zero).astype(HOT)
        tally = lax.dot_general(
            row_hot, low_hot, (((1,), (1,)), ((), ())), preferred_element_type=jnp.float32
        ).astype(jnp.bfloat16)
        base = pl.multiple_of(unit * rows, rows)
        for top in range(tops):
            tally_ref[pl.ds(base, rows), top * LANES : (top + 1) * LANES] = tally[
                top * rows : (top + 1) * rows
            ]
        return 0

    chunks = out_sems.shape[0]
    span = units // chunks
    stores = []
    for chunk in range(chunks):
        lax.fori_loop(chunk * span, (chunk + 1) * span, unit_step, 0, unroll=16)
        part = pl.ds(chunk * span * rows, span * rows)
        begin = 0
        for spot, tally_hbm in enumerate(tally_hbms):
            size = tally_hbm.shape[1]
            store = pltpu.make_async_copy(
                tally_ref.at[part, pl.ds(begin, size)],
                tally_hbm.at[part],
                out_sems.at[chunk, spot],
            )
            store.start()
            stores.append(store)
            begin += size
    for load in loads[4:]:
        load.wait()
    grouped_ref[...] = jnp.dot(
        tally_ref[...], pressure_ref[...], preferred_element_type=jnp.float32
    )
    core = core_ref[0]
    share = mine_ref.shape[1]
    for part in range(UNIT):
        sums = [None] * (places + 1)
        for place in range(places):
            first = part * combos + place * kinds
            picked = [
                grouped_ref[pl.ds(first + kind, units, stride=rows), :] for kind in range(kinds)
            ]
            wide = jnp.concatenate(
                [
                    jnp.concatenate([g[:, w * voxels : (w + 1) * voxels] for g in picked], axis=1)
                    for w in range(2)
                ],
                axis=0,
            )
            taps = jnp.dot(
                jnp.concatenate(split_parts(wide, 3), axis=0),
                kernel_ref[...],
                preferred_element_type=jnp.float32,
            )
            count = 2 * units
            taps = taps[:count] + (taps[count : 2 * count] + taps[2 * count :])
            for half in range(2):
                piece = taps[:, half * frame : (half + 1) * frame]
                spot = place + half
                sums[spot] = piece if sums[spot] is None else sums[spot] + piece
        total = jnp.concatenate(sums, axis=1)
        total = jnp.concatenate([total[:units], total[units:]], axis=1)
        pairs = units // (2 * share)
        for pair in range(pairs):
            even = total[2 * pair * share : (2 * pair + 1) * share]
            odd = total[(2 * pair + 1) * share : (2 * pair + 2) * share]
            mine_ref[part * pairs + pair] = jnp.where(core == 0, even, odd)
            other_ref[part * pairs + pair] = jnp.where(core == 0, odd, even)
    for store in stores:
        store.wait()


def forward(blocks, frames, classes, counts, pressure, kern_rows, kinds, places, time_len):
    slots, sensors = blocks.shape
    combos = kinds * places
    block_count = pressure.shape[0]
    slabs = lax.axis_size("slab")
    core = (lax.axis_index("slab") % 2).reshape(1)
    anywhere = pl.BlockSpec(memory_space=pltpu.HBM)
    vmem = pl.BlockSpec(memory_space=pltpu.VMEM)
    half = (slabs // 2, sensors // slabs, 2 * time_len)
    tallies = [
        jax.ShapeDtypeStruct((sensors * combos, block_count * cuts // sum(SPANS)), jnp.bfloat16)
        for cuts in SPANS
    ]
    operands = (blocks, frames, classes, counts, pressure, kern_rows)
    *tallies, mine, other = pl.pallas_call(
        functools.partial(forward_kernel, kinds, places),
        in_specs=[pl.BlockSpec(memory_space=pltpu.SMEM)] + [anywhere] * 6,
        out_specs=[anywhere] * len(SPANS) + [vmem, vmem],
        out_shape=tallies
        + [
            jax.ShapeDtypeStruct(half, jnp.float32),
            jax.ShapeDtypeStruct(half, jnp.float32),
        ],
        scratch_shapes=[pltpu.VMEM(operand.shape, operand.dtype) for operand in operands]
        + [
            pltpu.VMEM((sensors * combos, block_count), jnp.bfloat16),
            pltpu.VMEM((sensors // UNIT, UNIT * slots), jnp.int32),
            pltpu.VMEM((sensors * combos, pressure.shape[1]), jnp.float32),
            pltpu.SemaphoreType.DMA((len(operands),)),
            pltpu.SemaphoreType.DMA((2, len(SPANS))),
        ],
        compiler_params=pltpu.CompilerParams(vmem_limit_bytes=48 << 20),
        name="forward",
    )(core, *[in_hbm(operand) for operand in operands])
    return tallies, mine, other


def fill_responses(kinds, places, order_ref, piece_refs, kernel_ref, resp_ref, back_ref, wide_ref):
    combos = kinds * places
    rows = UNIT * combos
    share = piece_refs[0].shape[0]
    sensors = back_ref.shape[0]
    units = sensors // UNIT
    time_len = back_ref.shape[1] // 2
    taps = kernel_ref.shape[1]
    frame = taps // 2
    width = wide_ref.shape[1]
    voxels = width // 2
    for spot, piece_ref in enumerate(piece_refs):
        start = pl.multiple_of(order_ref[spot] * share, share)
        back_ref[pl.ds(start, share), :] = piece_ref[...]
    for place in range(places):
        waves = []
        for w in range(2):
            start = w * time_len + place * frame
            waves.append(
                lax.dot_general(
                    back_ref[:, start : start + taps],
                    kernel_ref[...],
                    (((1,), (1,)), ((), ())),
                    preferred_element_type=jnp.float32,
                )
            )
        for kind in range(kinds):
            cut = slice(kind * voxels, (kind + 1) * voxels)
            both = jnp.concatenate([waves[0][:, cut], waves[1][:, cut]], axis=1)
            for part in range(UNIT):
                first = part * combos + place * kinds + kind
                wide_ref[pl.ds(first, units, stride=rows), :] = both[
                    part * units : (part + 1) * units
                ]
    high, low = split_parts(wide_ref[...].T, 2)
    resp_ref[:width] = high
    resp_ref[width:] = low


def backward_kernel(kinds, places, pieces, own_ref, tally_hbm, *refs):
    if pieces:
        order_ref, *piece_refs = refs[: pieces + 1]
        kernel_ref, resp_ref, kept_ref, *code_refs = refs[pieces + 1 : -5]
        tally_ref, grad_ref, sems, back_ref, wide_ref = refs[-5:]
    else:
        tally_ref = tally_hbm
        resp_ref, kept_ref, *code_refs, grad_ref = refs
    groups, share, span = grad_ref.shape
    loads = [None]
    if pieces:
        cuts = sems.shape[0]
        loads = []
        for cut in range(cuts):
            here = pl.ds(cut * (span // cuts), span // cuts)
            loads.append(
                pltpu.make_async_copy(tally_hbm.at[:, here], tally_ref.at[:, here], sems.at[cut])
            )
            loads[-1].start()
    if pieces:
        fill_responses(
            kinds, places, order_ref, piece_refs, kernel_ref, resp_ref, back_ref, wide_ref
        )
    width = groups * share
    for cut, load in enumerate(loads):
        if load is not None:
            load.wait()
        here = slice(cut * (span // len(loads)), (cut + 1) * (span // len(loads)))
        both = jnp.dot(resp_ref[...], tally_ref[:, here], preferred_element_type=jnp.float32)
        both = both[:width] + both[width:]
        for group in range(groups):
            grad_ref[group, :, here] = both[group * share : (group + 1) * share]
    own = own_ref[0]
    kept_ref[...] = grad_ref[own]
    lanes = code_refs[0].shape[1] - span
    lane = lax.broadcasted_iota(jnp.int32, (share, lanes), 1)
    for step, code_ref in enumerate(code_refs, 1):
        levels = jnp.zeros((share, lanes), jnp.int32)
        for spot in range(span // GRAIN):
            cut = slice(spot * GRAIN, (spot + 1) * GRAIN)
            block = grad_ref[own ^ step, :, cut]
            top = jnp.maximum(jnp.max(jnp.abs(block), axis=1, keepdims=True), TINY)
            level = jnp.minimum(jnp.floor(jnp.log(top) * RATE) + 2.0, CODE)
            code = block * jnp.exp(level * (-1.0 / RATE)) * CODE
            code_ref[:, cut] = jnp.floor(code + 0.5).astype(jnp.int32).astype(jnp.int16)
            levels = jnp.where(lane == spot, level.astype(jnp.int32), levels)
        code_ref[:, span:] = levels.astype(jnp.int16)


def backward(own, tally, width, resp=None, order=None, pieces=(), kern_rows=None, combos=None):
    groups = lax.axis_size("sens")
    share, (rows, span) = width // groups, tally.shape
    vmem = pl.BlockSpec(memory_space=pltpu.VMEM)
    smem = pl.BlockSpec(memory_space=pltpu.SMEM)
    hbm = pl.BlockSpec(memory_space=pltpu.HBM)
    out_shape = [jax.ShapeDtypeStruct((share, span), jnp.float32)] + [
        jax.ShapeDtypeStruct((share, span + 128), jnp.int16)
    ] * (groups - 1)
    scratch = [pltpu.VMEM((groups, share, span), jnp.float32)]
    if resp is None:
        tally = in_hbm(tally)
        scratch = [
            pltpu.VMEM((rows, span), tally.dtype),
            *scratch,
            pltpu.SemaphoreType.DMA((span // CUT,)),
        ]
        operands = (order, *pieces, pltpu.with_memory_space_constraint(kern_rows, pltpu.VMEM))
        specs = [smem] + [vmem] * (len(pieces) + 1)
        out_shape = [jax.ShapeDtypeStruct((2 * width, rows), jnp.bfloat16)] + out_shape
        length = pieces[0].shape[1]
        sensors = pieces[0].shape[0] * len(pieces)
        scratch += [
            pltpu.VMEM((sensors, length), jnp.bfloat16),
            pltpu.VMEM((rows, width), jnp.float32),
        ]
    else:
        tally, hbm = pltpu.with_memory_space_constraint(tally, pltpu.VMEM), vmem
        operands, specs = (resp,), [vmem]
    outs = pl.pallas_call(
        functools.partial(backward_kernel, *(combos or (0, 0)), len(pieces)),
        in_specs=[smem, hbm] + specs,
        out_specs=[vmem] * len(out_shape),
        out_shape=out_shape,
        scratch_shapes=scratch,
        compiler_params=pltpu.CompilerParams(vmem_limit_bytes=24 << 20),
        cost_estimate=pl.CostEstimate(
            flops=4 * width * rows * span * 1, bytes_accessed=2 * rows * span, transcendentals=0
        ),
        name="backward",
    )(own, tally, *operands)
    if resp is None:
        resp, *outs = outs
    kept, *codes = outs
    received = []
    for step in range(groups - 1, 0, -1):
        pairs = [(q, q ^ step) for q in range(groups)]
        received.append(lax.ppermute(codes[step - 1], "sens", pairs))
    return resp, [kept, *received]


def finish_kernel(*refs):
    part_refs, out_ref = refs[:-1], refs[-1]
    count = len(part_refs) // len(SPANS)
    begin = 0
    for part in range(len(SPANS)):
        kept_ref, *code_refs = part_refs[part * count : (part + 1) * count]
        span = kept_ref.shape[1]
        for spot in range(span // GRAIN):
            cut = slice(spot * GRAIN, (spot + 1) * GRAIN)
            total = kept_ref[:, cut]
            for code_ref in code_refs:
                level = code_ref[:, span:].astype(jnp.int32).astype(jnp.float32)[:, spot : spot + 1]
                scale = jnp.exp(level * (1.0 / RATE)) * (1.0 / CODE)
                total = total + code_ref[:, cut].astype(jnp.int32).astype(jnp.float32) * scale
            out_ref[:, begin : begin + GRAIN] = total
            begin += GRAIN


def finish(parts, block_count):
    return pl.pallas_call(
        finish_kernel,
        out_shape=jax.ShapeDtypeStruct((parts[0].shape[0], block_count), jnp.float32),
        compiler_params=pltpu.CompilerParams(vmem_limit_bytes=8 << 20),
        name="finish",
    )(*parts)


def scatter_slab(mine, other, gains):
    slabs = lax.axis_size("slab")
    chips = slabs // 2
    place = lax.axis_index("slab")
    chip = place // 2
    paired = mine + lax.ppermute(other, "slab", [(j, j ^ 1) for j in range(slabs)])
    paired, gains = lax.optimization_barrier((paired, gains))
    received = [lax.dynamic_index_in_dim(paired, chip, 0, keepdims=False)]
    for step in (2, 1, 3) if chips == 4 else range(1, chips):
        block = lax.dynamic_index_in_dim(paired, chip ^ step, 0, keepdims=False)
        received.append(
            lax.ppermute(block, "slab", [(j, j ^ (2 * step)) for j in range(slabs)])
        )
    return received, gains


def refine_kernel(*refs):
    *piece_refs, matrix_ref, measured_ref, residual_ref, back_ref = refs
    total = piece_refs[0][...]
    for piece_ref in piece_refs[1:]:
        total = total + piece_ref[...]
    share, length = total.shape
    half = length // 2
    rows = jnp.concatenate([total[:, :half], total[:, half:]], axis=0)
    dot = functools.partial(
        jnp.dot, precision=lax.Precision.HIGHEST, preferred_element_type=jnp.float32
    )
    residual = dot(rows, matrix_ref[...]) - measured_ref[...]
    residual_ref[...] = residual
    back = dot(residual, matrix_ref[...]).astype(jnp.bfloat16)
    back_ref[:, :half] = back[:share]
    back_ref[:, half:] = back[share:]


def refine(received, matrix, measured):
    share, length = received[0].shape
    return pl.pallas_call(
        refine_kernel,
        out_shape=[
            jax.ShapeDtypeStruct(measured.shape, jnp.float32),
            jax.ShapeDtypeStruct((share, length), jnp.bfloat16),
        ],
        compiler_params=pltpu.CompilerParams(vmem_limit_bytes=12 << 20),
        name="refine",
    )(*[pltpu.with_memory_space_constraint(piece, pltpu.VMEM) for piece in received], matrix, measured)


def gather_slab(share):
    slabs = lax.axis_size("slab")
    place = lax.axis_index("slab")
    pieces, order = [share], [place]
    for step in range(slabs // 2 - 1, 0, -1):
        pieces.append(lax.ppermute(share, "slab", [(j, j ^ (2 * step)) for j in range(slabs)]))
        order.append(place ^ (2 * step))
    for spot in range(slabs // 2):
        pieces.append(lax.ppermute(pieces[spot], "slab", [(j, j ^ 1) for j in range(slabs)]))
        order.append(order[spot] ^ 1)
    return pieces, jnp.stack(order).astype(jnp.int32)


def per_device(pressure, kernels, filter_gains, measured, blocks, frames, classes, counts):
    kinds, voxels, taps = kernels.shape
    block_count, width = pressure.shape
    frame = taps // 2
    time_len = filter_gains.shape[0]
    places = time_len // frame - 1
    combos = kinds * places
    sensors, slots = blocks.shape[0], blocks.shape[2]
    share = sensors // lax.axis_size("slab")

    kern_rows = kernels.reshape(kinds * voxels, taps)

    tallies, mine, other = forward(
        blocks[:, 0, :].T,
        frames[:, 0, :].T,
        classes[:, 0, :].T,
        counts.T,
        pressure,
        kern_rows,
        kinds,
        places,
        time_len,
    )
    received, gains = scatter_slab(mine, other, filter_gains)
    matrix, kern_fast = filter_matrix(gains, kern_rows)
    measured_share = lax.dynamic_slice_in_dim(measured, lax.axis_index("slab") * share, share, 0)
    measured_share = measured_share.transpose(1, 0, 2).reshape(2 * share, time_len)
    residual, back = refine(received, matrix, measured_share)
    residual = residual.reshape(2, share, time_len).transpose(1, 0, 2)
    pieces, order = gather_slab(back)
    own = lax.axis_index("sens").reshape(1)
    resp, parts = backward(
        own, tallies[0], width, None, order, pieces, kern_fast, (kinds, places)
    )
    parts = parts + backward(own, tallies[1], width, resp)[1]
    gradient = finish(parts, block_count).T
    return (residual, gradient)


def solution(mesh):
    return jax.shard_map(
        per_device,
        mesh=mesh,
        in_specs=(
            P("slab", None),
            P(),
            P(),
            P("sens", None, None),
            P("sens", "slab", None),
            P("sens", "slab", None),
            P("sens", "slab", None),
            P("sens", "slab"),
        ),
        out_specs=(P(("sens", "slab"), None, None), P("slab", "sens")),
        check_vma=False,
    )
```

```python
import functools
import math

import jax
import jax.numpy as jnp
import numpy as np
from jax import lax
from jax.experimental import pallas as pl
from jax.experimental.pallas import tpu as pltpu
from jax.sharding import PartitionSpec as P

LANES = 256
UNIT = 4
HOT = jnp.float8_e4m3fn
CODE = 32766.0
TINY = 1e-37
RATE = 256 / math.log(2.0)
GRAIN = 512
SPANS = (4, 4)
CUT = 512


def in_hbm(array):
    return pltpu.with_memory_space_constraint(array, pltpu.HBM)


def to_bf16(array):
    return array.astype(jnp.float32).astype(jnp.bfloat16)


def filter_kernel(gains_hbm, cosine_hbm, kernel_hbm, matrix_ref, fast_ref, *refs):
    gains_ref, cosine_ref, sems = refs
    pairs = [(gains_hbm, gains_ref), (cosine_hbm, cosine_ref), (kernel_hbm, fast_ref)]
    copies = [
        pltpu.make_async_copy(source, target, sems.at[spot])
        for spot, (source, target) in enumerate(pairs)
    ]
    for copy in copies:
        copy.start()
    for copy in copies[:2]:
        copy.wait()
    time_len = cosine_ref.shape[0]
    row = jnp.dot(
        jnp.broadcast_to(gains_ref[...], (8, time_len)),
        cosine_ref[...],
        precision=lax.Precision.HIGHEST,
        preferred_element_type=jnp.float32,
    )
    wide = jnp.broadcast_to(row[:1] / time_len, (time_len, time_len))
    matrix_ref[...] = pltpu.roll(wide, 0, axis=1, stride=1, stride_axis=0)
    for copy in copies[2:]:
        copy.wait()


def filter_matrix(filter_gains, kern_rows):
    time_len = filter_gains.shape[0]
    ids = np.arange(time_len)
    cosine = np.cos(np.outer(ids, ids) % time_len * (2.0 * math.pi / time_len))
    operands = (filter_gains[None, :], jnp.asarray(cosine, jnp.float32), kern_rows)
    return pl.pallas_call(
        filter_kernel,
        in_specs=[pl.BlockSpec(memory_space=pltpu.HBM)] * 3,
        out_specs=[pl.BlockSpec(memory_space=pltpu.VMEM)] * 2,
        out_shape=[
            pltpu.VMEM((time_len, time_len), jnp.float32),
            pltpu.VMEM(kern_rows.shape, kern_rows.dtype),
        ],
        scratch_shapes=[
            pltpu.VMEM((1, time_len), jnp.float32),
            pltpu.VMEM((time_len, time_len), jnp.float32),
            pltpu.SemaphoreType.DMA((3,)),
        ],
        compiler_params=pltpu.CompilerParams(vmem_limit_bytes=8 << 20),
        name="filter_matrix",
    )(*[in_hbm(operand) for operand in operands])


def split_parts(array, count):
    parts = []
    for _ in range(count):
        part = array.astype(jnp.bfloat16)
        parts.append(part)
        array = array - part.astype(jnp.float32)
    return parts


def forward_kernel(
    kinds,
    places,
    core_ref,
    blocks_hbm,
    frames_hbm,
    classes_hbm,
    counts_hbm,
    pressure_hbm,
    kernel_hbm,
    *refs,
):
    tally_hbms = refs[: len(SPANS)]
    (
        mine_ref,
        other_ref,
        blocks_ref,
        frames_ref,
        classes_ref,
        counts_ref,
        pressure_ref,
        kernel_ref,
        tally_ref,
        code_ref,
        grouped_ref,
        in_sems,
        out_sems,
    ) = refs[len(SPANS) :]
    loads = [
        pltpu.make_async_copy(source, target, in_sems.at[spot])
        for spot, (source, target) in enumerate(
            (
                (blocks_hbm, blocks_ref),
                (frames_hbm, frames_ref),
                (classes_hbm, classes_ref),
                (counts_hbm, counts_ref),
                (pressure_hbm, pressure_ref),
                (kernel_hbm, kernel_ref),
            )
        )
    ]
    for load in loads:
        load.start()
    for load in loads[:4]:
        load.wait()
    combos = kinds * places
    rows = UNIT * combos
    block_count = pressure_ref.shape[0]
    tops = block_count // LANES
    slots, sensors = blocks_ref.shape
    units = sensors // UNIT
    voxels = pressure_ref.shape[1] // 2
    frame = kernel_ref.shape[1] // 2

    block_ids = blocks_ref[...]
    lane = lax.broadcasted_iota(jnp.int32, (slots, sensors), 1) // units
    row_ids = lane * combos + frames_ref[...] * kinds + classes_ref[...]
    live = lax.broadcasted_iota(jnp.int32, (slots, sensors), 0) < counts_ref[...]
    code = jnp.where(live, row_ids * block_count + block_ids, -1).T
    code_ref[...] = jnp.concatenate(
        [code[part * units : (part + 1) * units] for part in range(UNIT)], axis=1
    )

    width = UNIT * slots
    step = 16
    row_iota = to_bf16(lax.broadcasted_iota(jnp.int32, (rows, width), 0))
    low_iota = to_bf16(lax.broadcasted_iota(jnp.int32, (LANES, width), 0))
    one, zero = jnp.ones((), jnp.bfloat16), jnp.zeros((), jnp.bfloat16)
    blank = jnp.zeros((step, width // 2), jnp.bfloat16)
    shift = LANES.bit_length() - 1
    depth = block_count.bit_length() - 1

    def unit_step(unit, _):
        code = code_ref[pl.ds(unit, 1), :]
        row_code = to_bf16(lax.shift_right_arithmetic(code, depth))
        top_code = to_bf16(lax.shift_right_arithmetic(code & (block_count - 1), shift))
        low_code = to_bf16(code & (LANES - 1))
        picked = jnp.where(row_iota == row_code, one, zero)
        top_code = jnp.broadcast_to(top_code, (step, width))
        row_hot = []
        for top in range(tops):
            here = top_code == jnp.bfloat16(top)
            for cut in range(0, rows, step):
                halves = []
                for side in range(2):
                    lanes = slice(side * width // 2, (side + 1) * width // 2)
                    if cut + step <= side * rows // 2 or cut >= (side + 1) * rows // 2:
                        halves.append(blank)
                    else:
                        block = picked[cut : cut + step, lanes]
                        halves.append(jnp.where(here[:, lanes], block, zero))
                row_hot.append(jnp.concatenate(halves, axis=1))
        row_hot = jnp.concatenate(row_hot, axis=0).astype(HOT)
        low_hot = jnp.where(low_iota == low_code, one, zero).astype(HOT)
        tally = lax.dot_general(
            row_hot, low_hot, (((1,), (1,)), ((), ())), preferred_element_type=jnp.float32
        ).astype(jnp.bfloat16)
        base = pl.multiple_of(unit * rows, rows)
        for top in range(tops):
            tally_ref[pl.ds(base, rows), top * LANES : (top + 1) * LANES] = tally[
                top * rows : (top + 1) * rows
            ]
        return 0

    chunks = out_sems.shape[0]
    span = units // chunks
    stores = []
    for chunk in range(chunks):
        lax.fori_loop(chunk * span, (chunk + 1) * span, unit_step, 0, unroll=16)
        part = pl.ds(chunk * span * rows, span * rows)
        begin = 0
        for spot, tally_hbm in enumerate(tally_hbms):
            size = tally_hbm.shape[1]
            store = pltpu.make_async_copy(
                tally_ref.at[part, pl.ds(begin, size)],
                tally_hbm.at[part],
                out_sems.at[chunk, spot],
            )
            store.start()
            stores.append(store)
            begin += size
    for load in loads[4:]:
        load.wait()
    grouped_ref[...] = jnp.dot(
        tally_ref[...], pressure_ref[...], preferred_element_type=jnp.float32
    )
    core = core_ref[0]
    share = mine_ref.shape[1]
    for part in range(UNIT):
        sums = [None] * (places + 1)
        for place in range(places):
            first = part * combos + place * kinds
            picked = [
                grouped_ref[pl.ds(first + kind, units, stride=rows), :] for kind in range(kinds)
            ]
            wide = jnp.concatenate(
                [
                    jnp.concatenate([g[:, w * voxels : (w + 1) * voxels] for g in picked], axis=1)
                    for w in range(2)
                ],
                axis=0,
            )
            taps = jnp.dot(
                jnp.concatenate(split_parts(wide, 3), axis=0),
                kernel_ref[...],
                preferred_element_type=jnp.float32,
            )
            count = 2 * units
            taps = taps[:count] + (taps[count : 2 * count] + taps[2 * count :])
            for half in range(2):
                piece = taps[:, half * frame : (half + 1) * frame]
                spot = place + half
                sums[spot] = piece if sums[spot] is None else sums[spot] + piece
        total = jnp.concatenate(sums, axis=1)
        total = jnp.concatenate([total[:units], total[units:]], axis=1)
        pairs = units // (2 * share)
        for pair in range(pairs):
            even = total[2 * pair * share : (2 * pair + 1) * share]
            odd = total[(2 * pair + 1) * share : (2 * pair + 2) * share]
            mine_ref[part * pairs + pair] = jnp.where(core == 0, even, odd)
            other_ref[part * pairs + pair] = jnp.where(core == 0, odd, even)
    for store in stores:
        store.wait()


def forward(blocks, frames, classes, counts, pressure, kern_rows, kinds, places, time_len):
    slots, sensors = blocks.shape
    combos = kinds * places
    block_count = pressure.shape[0]
    slabs = lax.axis_size("slab")
    core = (lax.axis_index("slab") % 2).reshape(1)
    anywhere = pl.BlockSpec(memory_space=pltpu.HBM)
    vmem = pl.BlockSpec(memory_space=pltpu.VMEM)
    half = (slabs // 2, sensors // slabs, 2 * time_len)
    tallies = [
        jax.ShapeDtypeStruct((sensors * combos, block_count * cuts // sum(SPANS)), jnp.bfloat16)
        for cuts in SPANS
    ]
    operands = (blocks, frames, classes, counts, pressure, kern_rows)
    *tallies, mine, other = pl.pallas_call(
        functools.partial(forward_kernel, kinds, places),
        in_specs=[pl.BlockSpec(memory_space=pltpu.SMEM)] + [anywhere] * 6,
        out_specs=[anywhere] * len(SPANS) + [vmem, vmem],
        out_shape=tallies
        + [
            jax.ShapeDtypeStruct(half, jnp.float32),
            jax.ShapeDtypeStruct(half, jnp.float32),
        ],
        scratch_shapes=[pltpu.VMEM(operand.shape, operand.dtype) for operand in operands]
        + [
            pltpu.VMEM((sensors * combos, block_count), jnp.bfloat16),
            pltpu.VMEM((sensors // UNIT, UNIT * slots), jnp.int32),
            pltpu.VMEM((sensors * combos, pressure.shape[1]), jnp.float32),
            pltpu.SemaphoreType.DMA((len(operands),)),
            pltpu.SemaphoreType.DMA((2, len(SPANS))),
        ],
        compiler_params=pltpu.CompilerParams(vmem_limit_bytes=48 << 20),
        name="forward",
    )(core, *[in_hbm(operand) for operand in operands])
    return tallies, mine, other


def fill_responses(kinds, places, order_ref, piece_refs, kernel_ref, resp_ref, back_ref, wide_ref):
    combos = kinds * places
    rows = UNIT * combos
    share = piece_refs[0].shape[0]
    sensors = back_ref.shape[0]
    units = sensors // UNIT
    time_len = back_ref.shape[1] // 2
    taps = kernel_ref.shape[1]
    frame = taps // 2
    width = wide_ref.shape[1]
    voxels = width // 2
    for spot, piece_ref in enumerate(piece_refs):
        start = pl.multiple_of(order_ref[spot] * share, share)
        back_ref[pl.ds(start, share), :] = piece_ref[...]
    for place in range(places):
        waves = []
        for w in range(2):
            start = w * time_len + place * frame
            waves.append(
                lax.dot_general(
                    back_ref[:, start : start + taps],
                    kernel_ref[...],
                    (((1,), (1,)), ((), ())),
                    preferred_element_type=jnp.float32,
                )
            )
        for kind in range(kinds):
            cut = slice(kind * voxels, (kind + 1) * voxels)
            both = jnp.concatenate([waves[0][:, cut], waves[1][:, cut]], axis=1)
            for part in range(UNIT):
                first = part * combos + place * kinds + kind
                wide_ref[pl.ds(first, units, stride=rows), :] = both[
                    part * units : (part + 1) * units
                ]
    high, low = split_parts(wide_ref[...].T, 2)
    resp_ref[:width] = high
    resp_ref[width:] = low


def backward_kernel(kinds, places, pieces, own_ref, tally_hbm, *refs):
    if pieces:
        order_ref, *piece_refs = refs[: pieces + 1]
        kernel_ref, resp_ref, kept_ref, *code_refs = refs[pieces + 1 : -5]
        tally_ref, grad_ref, sems, back_ref, wide_ref = refs[-5:]
    else:
        tally_ref = tally_hbm
        resp_ref, kept_ref, *code_refs, grad_ref = refs
    groups, share, span = grad_ref.shape
    loads = [None]
    if pieces:
        cuts = sems.shape[0]
        loads = []
        for cut in range(cuts):
            here = pl.ds(cut * (span // cuts), span // cuts)
            loads.append(
                pltpu.make_async_copy(tally_hbm.at[:, here], tally_ref.at[:, here], sems.at[cut])
            )
            loads[-1].start()
    if pieces:
        fill_responses(
            kinds, places, order_ref, piece_refs, kernel_ref, resp_ref, back_ref, wide_ref
        )
    width = groups * share
    for cut, load in enumerate(loads):
        if load is not None:
            load.wait()
        here = slice(cut * (span // len(loads)), (cut + 1) * (span // len(loads)))
        both = jnp.dot(resp_ref[...], tally_ref[:, here], preferred_element_type=jnp.float32)
        both = both[:width] + both[width:]
        for group in range(groups):
            grad_ref[group, :, here] = both[group * share : (group + 1) * share]
    own = own_ref[0]
    kept_ref[...] = grad_ref[own]
    lanes = code_refs[0].shape[1] - span
    lane = lax.broadcasted_iota(jnp.int32, (share, lanes), 1)
    for step, code_ref in enumerate(code_refs, 1):
        levels = jnp.zeros((share, lanes), jnp.int32)
        for spot in range(span // GRAIN):
            cut = slice(spot * GRAIN, (spot + 1) * GRAIN)
            block = grad_ref[own ^ step, :, cut]
            top = jnp.maximum(jnp.max(jnp.abs(block), axis=1, keepdims=True), TINY)
            level = jnp.minimum(jnp.floor(jnp.log(top) * RATE) + 2.0, CODE)
            code = block * jnp.exp(level * (-1.0 / RATE)) * CODE
            code_ref[:, cut] = jnp.floor(code + 0.5).astype(jnp.int32).astype(jnp.int16)
            levels = jnp.where(lane == spot, level.astype(jnp.int32), levels)
        code_ref[:, span:] = levels.astype(jnp.int16)


def backward(own, tally, width, resp=None, order=None, pieces=(), kern_rows=None, combos=None):
    groups = lax.axis_size("sens")
    share, (rows, span) = width // groups, tally.shape
    vmem = pl.BlockSpec(memory_space=pltpu.VMEM)
    smem = pl.BlockSpec(memory_space=pltpu.SMEM)
    hbm = pl.BlockSpec(memory_space=pltpu.HBM)
    out_shape = [jax.ShapeDtypeStruct((share, span), jnp.float32)] + [
        jax.ShapeDtypeStruct((share, span + 128), jnp.int16)
    ] * (groups - 1)
    scratch = [pltpu.VMEM((groups, share, span), jnp.float32)]
    if resp is None:
        tally = in_hbm(tally)
        scratch = [
            pltpu.VMEM((rows, span), tally.dtype),
            *scratch,
            pltpu.SemaphoreType.DMA((span // CUT,)),
        ]
        operands = (order, *pieces, pltpu.with_memory_space_constraint(kern_rows, pltpu.VMEM))
        specs = [smem] + [vmem] * (len(pieces) + 1)
        out_shape = [jax.ShapeDtypeStruct((2 * width, rows), jnp.bfloat16)] + out_shape
        length = pieces[0].shape[1]
        sensors = pieces[0].shape[0] * len(pieces)
        scratch += [
            pltpu.VMEM((sensors, length), jnp.bfloat16),
            pltpu.VMEM((rows, width), jnp.float32),
        ]
    else:
        tally, hbm = pltpu.with_memory_space_constraint(tally, pltpu.VMEM), vmem
        operands, specs = (resp,), [vmem]
    outs = pl.pallas_call(
        functools.partial(backward_kernel, *(combos or (0, 0)), len(pieces)),
        in_specs=[smem, hbm] + specs,
        out_specs=[vmem] * len(out_shape),
        out_shape=out_shape,
        scratch_shapes=scratch,
        compiler_params=pltpu.CompilerParams(vmem_limit_bytes=24 << 20),
        cost_estimate=pl.CostEstimate(
            flops=4 * width * rows * span * 1, bytes_accessed=2 * rows * span, transcendentals=0
        ),
        name="backward",
    )(own, tally, *operands)
    if resp is None:
        resp, *outs = outs
    kept, *codes = outs
    received = []
    for step in range(groups - 1, 0, -1):
        pairs = [(q, q ^ step) for q in range(groups)]
        received.append(lax.ppermute(codes[step - 1], "sens", pairs))
    return resp, [kept, *received]


def finish_kernel(*refs):
    part_refs, out_ref = refs[:-1], refs[-1]
    count = len(part_refs) // len(SPANS)
    begin = 0
    for part in range(len(SPANS)):
        kept_ref, *code_refs = part_refs[part * count : (part + 1) * count]
        span = kept_ref.shape[1]
        for spot in range(span // GRAIN):
            cut = slice(spot * GRAIN, (spot + 1) * GRAIN)
            total = kept_ref[:, cut]
            for code_ref in code_refs:
                level = code_ref[:, span:].astype(jnp.int32).astype(jnp.float32)[:, spot : spot + 1]
                scale = jnp.exp(level * (1.0 / RATE)) * (1.0 / CODE)
                total = total + code_ref[:, cut].astype(jnp.int32).astype(jnp.float32) * scale
            out_ref[:, begin : begin + GRAIN] = total
            begin += GRAIN


def finish(parts, block_count):
    return pl.pallas_call(
        finish_kernel,
        out_shape=jax.ShapeDtypeStruct((parts[0].shape[0], block_count), jnp.float32),
        compiler_params=pltpu.CompilerParams(vmem_limit_bytes=8 << 20),
        name="finish",
    )(*parts)


def scatter_slab(mine, other, gains):
    slabs = lax.axis_size("slab")
    chips = slabs // 2
    place = lax.axis_index("slab")
    chip = place // 2
    paired = mine + lax.ppermute(other, "slab", [(j, j ^ 1) for j in range(slabs)])
    paired, gains = lax.optimization_barrier((paired, gains))
    received = [lax.dynamic_index_in_dim(paired, chip, 0, keepdims=False)]
    for step in (2, 1, 3) if chips == 4 else range(1, chips):
        block = lax.dynamic_index_in_dim(paired, chip ^ step, 0, keepdims=False)
        received.append(
            lax.ppermute(block, "slab", [(j, j ^ (2 * step)) for j in range(slabs)])
        )
    return received, gains


def refine_kernel(*refs):
    *piece_refs, matrix_ref, measured_ref, residual_ref, back_ref = refs
    total = piece_refs[0][...]
    for piece_ref in piece_refs[1:]:
        total = total + piece_ref[...]
    share, length = total.shape
    half = length // 2
    rows = jnp.concatenate([total[:, :half], total[:, half:]], axis=0)
    dot = functools.partial(
        jnp.dot, precision=lax.Precision.HIGHEST, preferred_element_type=jnp.float32
    )
    residual = dot(rows, matrix_ref[...]) - measured_ref[...]
    residual_ref[...] = residual
    back = dot(residual, matrix_ref[...]).astype(jnp.bfloat16)
    back_ref[:, :half] = back[:share]
    back_ref[:, half:] = back[share:]


def refine(received, matrix, measured):
    share, length = received[0].shape
    return pl.pallas_call(
        refine_kernel,
        out_shape=[
            jax.ShapeDtypeStruct(measured.shape, jnp.float32),
            jax.ShapeDtypeStruct((share, length), jnp.bfloat16),
        ],
        compiler_params=pltpu.CompilerParams(vmem_limit_bytes=12 << 20),
        name="refine",
    )(*[pltpu.with_memory_space_constraint(piece, pltpu.VMEM) for piece in received], matrix, measured)


def gather_slab(share):
    slabs = lax.axis_size("slab")
    place = lax.axis_index("slab")
    pieces, order = [share], [place]
    for step in range(slabs // 2 - 1, 0, -1):
        pieces.append(lax.ppermute(share, "slab", [(j, j ^ (2 * step)) for j in range(slabs)]))
        order.append(place ^ (2 * step))
    for spot in range(slabs // 2):
        pieces.append(lax.ppermute(pieces[spot], "slab", [(j, j ^ 1) for j in range(slabs)]))
        order.append(order[spot] ^ 1)
    return pieces, jnp.stack(order).astype(jnp.int32)


def per_device(pressure, kernels, filter_gains, measured, blocks, frames, classes, counts):
    kinds, voxels, taps = kernels.shape
    block_count, width = pressure.shape
    frame = taps // 2
    time_len = filter_gains.shape[0]
    places = time_len // frame - 1
    combos = kinds * places
    sensors, slots = blocks.shape[0], blocks.shape[2]
    share = sensors // lax.axis_size("slab")

    kern_rows = kernels.reshape(kinds * voxels, taps)

    tallies, mine, other = forward(
        blocks[:, 0, :].T,
        frames[:, 0, :].T,
        classes[:, 0, :].T,
        counts.T,
        pressure,
        kern_rows,
        kinds,
        places,
        time_len,
    )
    received, gains = scatter_slab(mine, other, filter_gains)
    matrix, kern_fast = filter_matrix(gains, kern_rows)
    measured_share = lax.dynamic_slice_in_dim(measured, lax.axis_index("slab") * share, share, 0)
    measured_share = measured_share.transpose(1, 0, 2).reshape(2 * share, time_len)
    residual, back = refine(received, matrix, measured_share)
    residual = residual.reshape(2, share, time_len).transpose(1, 0, 2)
    pieces, order = gather_slab(back)
    own = lax.axis_index("sens").reshape(1)
    resp, parts = backward(
        own, tallies[0], width, None, order, pieces, kern_fast, (kinds, places)
    )
    parts = parts + backward(own, tallies[1], width, resp)[1]
    gradient = finish(parts, block_count).T
    return (residual, gradient)


def solution(mesh):
    return jax.shard_map(
        per_device,
        mesh=mesh,
        in_specs=(
            P("slab", None),
            P(),
            P(),
            P("sens", None, None),
            P("sens", "slab", None),
            P("sens", "slab", None),
            P("sens", "slab", None),
            P("sens", "slab"),
        ),
        out_specs=(P(("sens", "slab"), None, None), P("slab", "sens")),
        check_vma=False,
    )
```
